256 devices in a mesh: leaf: 4 (over x_lo, core), row: 8 (over y, x_hi), col: 8 (over z).
Axes of the slice: x: 4 (x_hi: 2, x_lo: 2; x = x_hi * 2 + x_lo), y: 4, z: 8, core: 2. Of those that a mesh axis runs over, the one named last changes fastest.
Arguments:
- top_inverse: float32 [4096, 4096], P('row', ('leaf', 'col')), as said below
- pattern: int32 [4, 16], P('leaf'), may hold values from 0 to 31, as said below
- panel: float32 [4, 2048, 2048], P('leaf', None, 'col'), may hold values from -1.6 to 1.6
- diag_inverse: float32 [4, 2048, 2048], P('leaf', 'row', 'col'), as said below
Outputs:
- sigma_top: float32 [4096, 4096], P('row', ('leaf', 'col'))
- sigma_panel: float32 [4, 2048, 2048], P('leaf', 'row', 'col')
- sigma_diag: float32 [4, 2048, 2048], P('leaf', 'row', 'col')
The draws below stay inside these ranges and needn't reach their ends.
Inputs may be any that keep to these rules, and one draw needn't show every extreme that they name: `pattern`: each row holds 16 distinct block indices in rising order, among them 0 and 31. `top_inverse`: lower triangular with a positive diagonal. `diag_inverse`: each group's block is symmetric.
All inputs are finite; a program needn't handle non-finite values.
Results may differ from the reference program's by a relative error of at most 0.00016.
Values sent between devices are 32-bit elements; how exact they have to be, the bound alone decides.
A program may use at most 64 MiB of HBM per device.

```python
import math
import jax
import jax.numpy as jnp
from jax import lax

BLK = 128
NBA = 32
NS = 16
W = 2048
WA = 4096
SROWS = 2048
GROUPS = 4


def draw_pattern(key, part):

    def single(one_key):
        inner = jax.random.permutation(one_key, NBA - 2)[:NS - 2].astype(jnp.int32) + 1
        ends = jnp.array([0, NBA - 1], dtype=jnp.int32)
        return jnp.sort(jnp.concatenate([ends, inner]))
    keys = jax.random.split(jax.random.fold_in(key, 11), GROUPS)
    return jax.vmap(single)(keys).astype(jnp.int32)


def draw_top_inverse(key, part):
    first, second = jax.random.split(jax.random.fold_in(key, 23), 2)
    rows_idx = lax.broadcasted_iota(jnp.int32, (WA, WA), 0)
    cols_idx = lax.broadcasted_iota(jnp.int32, (WA, WA), 1)
    rough = jax.random.normal(first, (WA, WA), jnp.float32)
    diagonal = jnp.exp(jax.random.uniform(second, (WA, WA), jnp.float32, math.log(0.3), math.log(3.0)))
    lower = rough / math.sqrt(WA)
    result = jnp.where(rows_idx > cols_idx, lower, jnp.where(rows_idx == cols_idx, diagonal, 0.0))
    return result.astype(jnp.float32)


def draw_diag_inverse(key, part):
    first, second = jax.random.split(jax.random.fold_in(key, 37), 2)
    rough = jax.random.normal(first, (GROUPS, W, W), jnp.float32)
    symmetric = (rough + jnp.swapaxes(rough, 1, 2)) * (0.5 / math.sqrt(W)) * 3.0
    rows_idx = lax.broadcasted_iota(jnp.int32, (GROUPS, W, W), 1)
    cols_idx = lax.broadcasted_iota(jnp.int32, (GROUPS, W, W), 2)
    levels = jnp.exp(jax.random.uniform(second, (GROUPS, W, 1), jnp.float32, 0.0, math.log(3.0)))
    result = symmetric + jnp.where(rows_idx == cols_idx, levels, 0.0)
    return result.astype(jnp.float32)


def block_levels(key, shape, cuts, least, largest):
    loudness, own = 1.0, jax.random.fold_in(key, 6)
    for position, shards_of in cuts:
        steps = jnp.exp(jax.random.uniform(jax.random.fold_in(own, position), (shards_of,), jnp.float32, least / len(cuts), largest / len(cuts)))
        loudness = loudness * jnp.repeat(steps, shape[position] // shards_of).reshape([-1 if axis == position else 1 for axis in range(len(shape))])
    return loudness


def scatter_about(own_key, shape, width, limit, pieces=(), kind=jnp.bfloat16):
    level = block_levels(own_key, shape, pieces, -0.22, 0.18) if pieces else 1.0
    values = jax.random.normal(own_key, shape, jnp.float32) * width * level
    return jnp.minimum(jnp.maximum(values, -limit), limit).astype(kind)


def setup_inputs(seed: int = 0) -> dict:
    seeds = jax.random.split(jax.random.key(seed), 5)
    top_inverse = draw_top_inverse(jax.random.fold_in(seeds[4], 71), 0)
    pattern = draw_pattern(jax.random.fold_in(seeds[4], 71), 0)
    panel = scatter_about(seeds[2], (GROUPS, SROWS, W), 0.2, 1.6, ((0, 4), (2, 8)), jnp.float32)
    diag_inverse = draw_diag_inverse(jax.random.fold_in(seeds[4], 71), 0)
    return {"top_inverse": top_inverse, "pattern": pattern, "panel": panel, "diag_inverse": diag_inverse}


def reference(top_inverse, pattern, panel, diag_inverse):
    exact = lax.Precision.HIGHEST
    sigma_top = jnp.dot(top_inverse.T, top_inverse, precision=exact, preferred_element_type=jnp.float32)
    offsets = jnp.arange(BLK, dtype=jnp.int32)
    panels = []
    diagonals = []
    for group_id in range(GROUPS):
        rows_sel = (pattern[group_id][:, None].astype(jnp.int32) * BLK + offsets[None, :]).reshape(-1).astype(jnp.int32)
        sub_block = jnp.take(jnp.take(sigma_top, rows_sel, axis=0), rows_sel, axis=1)
        sig_panel = -jnp.dot(sub_block, panel[group_id], precision=exact, preferred_element_type=jnp.float32)
        sig_diag = diag_inverse[group_id] - jnp.dot(panel[group_id].T, sig_panel, precision=exact, preferred_element_type=jnp.float32)
        panels.append(sig_panel)
        diagonals.append(sig_diag)
    return sigma_top, jnp.stack(panels), jnp.stack(diagonals)
```

```python
import jax
import jax.numpy as jnp
from jax import lax
from jax.experimental import pallas as pl
from jax.experimental.pallas import tpu as pltpu
from jax.sharding import PartitionSpec as P

F32, BF16 = jnp.float32, jnp.bfloat16
NZ, NY = 8, 4


def split(x):
    hi = x.astype(BF16)
    return hi, (x - hi.astype(F32)).astype(BF16)


def mm(a, b):
    return jnp.dot(a, b, preferred_element_type=F32)


def kernel(
    pat, top, panel, diag, out_top, out_panel, out_diag,
    slab, shi, slo, jcat, ptr, pthi, ptlo, xt, xhi, xlo,
    tsl, tr1, tr2, acc, xtop, psl, pr1, pr2, px, sphi, splo,
    zs, zr, xs, xr, cs, cr, ts, tr, qs, qr, gs, gr, axs, axr,
):
    leaf, row, col = lax.axis_index("leaf"), lax.axis_index("row"), lax.axis_index("col")
    y, xh = row // 2, row % 2
    mod8 = lambda k: (col + k + 16) % 8
    z_dev = ({"col": mod8(1)}, {"col": mod8(-1)})
    y_dev = ({"row": (row + 2) % 8}, {"row": (row + 6) % 8})
    xl = (leaf + 2) % 4
    x_dev = {"leaf": xl}
    lc = leaf + 1 - 2 * (leaf % 2)
    lx = (lc + 2) % 4
    c_dev = {"leaf": lc}
    h_dev = {"row": row + 1 - 2 * xh}

    sem = pltpu.get_barrier_semaphore()
    peers = (*z_dev, *y_dev, x_dev, c_dev, h_dev)
    for dev in peers:
        pl.semaphore_signal(sem, inc=1, device_id=dev, device_id_type=pl.DeviceIdType.MESH)

    own = leaf * 8 + col
    for h in range(2):
        slab[own, h] = top[h * 256 : (h + 1) * 256, :].T
    pl.semaphore_wait(sem, len(peers))

    sent = []

    def copy(src, dst, ssem, rsem, dev):
        return pltpu.make_async_remote_copy(
            src_ref=src, dst_ref=dst, send_sem=ssem, recv_sem=rsem,
            device_id=dev, device_id_type=pl.DeviceIdType.MESH,
        )

    def send(src, dst, ssem, rsem, dev):
        desc = copy(src, dst, ssem, rsem, dev)
        desc.start()
        sent.append(desc)

    def arrived(dst, ssem, rsem, dev):
        copy(dst, dst, ssem, rsem, dev).wait_recv()

    def origin(p):
        return mod8(0 if p == 0 else -p if p < 4 else p - 3 if p < 7 else 4)

    def z_unit(d, t, u, hop):
        o = mod8((hop - t) if d == 0 else (t - hop))
        ref = slab.at[(leaf if u < 2 else xl) * 8 + o, 0 if u == 0 else 1]
        return ref.at[pl.ds(64 * d, 64)] if t == 4 else ref

    def z_send(d, t, u):
        ref = z_unit(d, t, u, 1)
        send(ref, ref, zs.at[d, t - 1, u], zr.at[d, t - 1, u], z_dev[d])

    def z_wait(d, t, u):
        arrived(z_unit(d, t, u, 0), zs.at[d, t - 1, u], zr.at[d, t - 1, u], z_dev[d])

    def x_send(p):
        ref = slab.at[leaf * 8 + origin(p), 0]
        send(ref, ref, xs.at[p], xr.at[p], x_dev)

    def x_wait(p):
        arrived(slab.at[xl * 8 + origin(p), 0], xs.at[p], xr.at[p], x_dev)

    halves = ((0, 0), (0, 1), (1, 1), (1, 0))

    def c_send(p, k):
        far, h = halves[k]
        ref = slab.at[(xl if far else leaf) * 8 + origin(p), h]
        send(ref, ref, cs.at[p, k], cr.at[p, k], c_dev)

    def c_wait(p):
        for k, (far, h) in enumerate(halves):
            arrived(slab.at[(lx if far else lc) * 8 + origin(p), h], cs.at[p, k], cr.at[p, k], c_dev)

    def top_slices(ps):
        for p in ps:
            c_wait(p)

        def body(i, _):
            q, rel = i // 4, i % 4
            zz = mod8((2 * q - 1) * ps[0]) if len(ps) > 1 else origin(ps[0])
            p = ps[0] + 3 * q
            b = ((y + rel) % 4) * 8 + zz
            a0h, a0l = split(slab[b, 0])
            a1h, a1l = split(slab[b, 1])
            shi[b, 0] = a0h
            shi[b, 1] = a1h
            slo[b, 0] = a0l
            slo[b, 1] = a1l
            wide = mm(a0h, jcat[0]) + mm(a1h, jcat[1])
            low = mm(a0l, jcat[0, :, :128]) + mm(a1l, jcat[1, :, :128])
            t = wide[:, :128] + wide[:, 128:] + low
            tsl[p, (2 * rel + 4) % 8] = t[:64]
            tsl[p, (2 * rel + 7) % 8] = t[64:]
            return 0

        lax.fori_loop(0, 4 * len(ps), body, 0)
        for p in ps:
            for d in range(2):
                send(tsl.at[p, pl.ds(2 * d, 2)], tr1.at[p, d], ts.at[p, d], tr.at[p, d], y_dev[d])

    def top_combine(ps):
        for p in ps:
            for d, slot in ((0, 6), (1, 5)):
                arrived(tr1.at[p, d], ts.at[p, d], tr.at[p, d], y_dev[d])
                tsl[p, slot] += tr1[p, d, d]
                send(tsl.at[p, slot], tr2.at[p, d], ts.at[p, 2 + d], tr.at[p, 2 + d], y_dev[d])

    def top_finish(ps):
        for p in ps:
            for d in range(2):
                arrived(tr2.at[p, d], ts.at[p, 2 + d], tr.at[p, 2 + d], y_dev[d])
            o = origin(p)
            acc[o, :64] = tsl[p, 4] + tr1[p, 1, 0] + tr2[p, 0]
            acc[o, 64:] = tsl[p, 7] + tr1[p, 0, 1] + tr2[p, 1]

    for d in range(2):
        z_send(d, 1, 0)
        z_send(d, 1, 1)
    ref = slab.at[own, 1]
    send(ref, ref, xs.at[8], xr.at[8], x_dev)
    x_send(0)
    c_send(0, 0)
    c_send(0, 1)
    for h in range(2):
        j_hi, j_lo = split(top[h * 256 : (h + 1) * 256, :])
        jcat[h, :, :128] = j_hi
        jcat[h, :, 128:] = j_lo
    arrived(slab.at[xl * 8 + col, 1], xs.at[8], xr.at[8], x_dev)
    for d in range(2):
        z_send(d, 1, 2)
    c_send(0, 2)

    def turn(i, _):
        block = panel[0, pl.ds(pl.multiple_of(i * 256, 256), 256), :].T
        hi, lo = split(block)
        pthi[i] = hi
        ptlo[i] = lo
        return 0

    lax.fori_loop(0, 8, turn, 0)
    ptr[col] = panel[0, pl.ds(pl.multiple_of(row * 256, 256), 256), :].T
    x_wait(0)
    c_send(0, 3)

    pairs = {0: (0,), 1: (1, 4), 2: (2, 5), 3: (3, 6), 4: (7,)}
    for t in range(1, 5):
        for u in range(3):
            for d in range(2):
                z_wait(d, t, u)
                if t < 4:
                    z_send(d, t + 1, u)
                    if u == 0:
                        x_send(pairs[t][d])
                    c_send(pairs[t][d], u)
            if t == 4:
                if u == 0:
                    x_send(7)
                c_send(7, u)
        if t >= 2:
            top_combine(pairs[t - 2])
        top_slices(pairs[t - 1])
        for p in pairs[t]:
            x_wait(p)
            c_send(p, 3)
        if t >= 3:
            top_finish(pairs[t - 3])

    def g_unit(d, t, hop):
        ref = ptr.at[mod8((hop - t) if d == 0 else (t - hop))]
        return ref.at[pl.ds(128 * d, 128)] if t == 4 else ref

    def g_send(t):
        for d in range(2):
            ref = g_unit(d, t, 1)
            send(ref, ref, gs.at[d, t - 1], gr.at[d, t - 1], z_dev[d])

    def g_wait(t):
        for d in range(2):
            arrived(g_unit(d, t, 0), gs.at[d, t - 1], gr.at[d, t - 1], z_dev[d])
        if t < 4:
            g_send(t + 1)

    g_send(1)
    top_combine(pairs[3])
    top_slices(pairs[4])
    top_finish(pairs[2])

    for h in range(2):
        xt[h] = jnp.zeros((256, 256), F32)

    def image(i, _):
        b0, b1 = pat[0, 2 * i], pat[0, 2 * i + 1]
        ph, p_lo = pthi[i], ptlo[i]
        for h in range(2):
            bh = jnp.concatenate([shi[b0, h], shi[b1, h]], axis=0)
            bl = jnp.concatenate([slo[b0, h], slo[b1, h]], axis=0)
            xt[h] += mm(ph, bh) + mm(p_lo, bh) + mm(ph, bl)
        return 0

    lax.fori_loop(0, 8, image, 0)
    for h in range(2):
        hi, lo = split(xt[h].T)
        xhi[h] = hi
        xlo[h] = lo
    top_combine(pairs[4])
    top_finish(pairs[3])

    def rel_of(k):
        return ((k + 1) // 2 + 2 * (1 - k % 2)) % 4

    def panel_part(s, k):
        j = 4 * ((y + rel_of(k)) % 4) + 2 * (k % 2) + s
        b = pat[0, j]
        total = jnp.zeros((128, 256), F32)
        for h in range(2):
            ah, al = shi[b, h], slo[b, h]
            total += mm(ah, xhi[h]) + mm(ah, xlo[h]) + mm(al, xhi[h])
        return total

    def diag_part(s, k):
        r = 2 * ((y + rel_of(k)) % 4) + k % 2
        ah, al = split(ptr[r, s * 128 : (s + 1) * 128, :])
        return mm(ah, sphi[...]) + mm(ah, splo[...]) + mm(al, sphi[...])

    def start(q, s, part):
        def body(k, _):
            psl[q, s, k] = part(s, k)
            return 0

        lax.fori_loop(0, 4, body, 0)
        for d in range(2):
            send(psl.at[q, s, pl.ds(2 * d, 2)], pr1.at[q, s, d], qs.at[q, s, d], qr.at[q, s, d], y_dev[d])
        lax.fori_loop(4, 8, body, 0)

    def combine(q, s):
        for d, slot in ((0, 6), (1, 5)):
            arrived(pr1.at[q, s, d], qs.at[q, s, d], qr.at[q, s, d], y_dev[d])
            psl[q, s, slot] += pr1[q, s, d, d]
            send(psl.at[q, s, slot], pr2.at[q, s, d], qs.at[q, s, 2 + d], qr.at[q, s, 2 + d], y_dev[d])

    def across(q, s):
        for d in range(2):
            arrived(pr2.at[q, s, d], qs.at[q, s, 2 + d], qr.at[q, s, 2 + d], y_dev[d])
        psl[q, s, 4] += pr1[q, s, 1, 0] + pr2[q, s, 0]
        psl[q, s, 7] += pr1[q, s, 0, 1] + pr2[q, s, 1]
        send(psl.at[q, s, 7 - 3 * xh], px.at[q, s], qs.at[q, s, 4], qr.at[q, s, 4], h_dev)

    def total(q, s):
        arrived(px.at[q, s], qs.at[q, s, 4], qr.at[q, s, 4], h_dev)
        return psl[q, s, 4 + 3 * xh] + px[q, s]

    start(0, 0, panel_part)
    start(0, 1, panel_part)
    g_wait(1)
    combine(0, 0)
    top_finish(pairs[4])
    ref = acc.at[pl.ds(4 * (1 - xh), 4)]
    send(ref, xtop, axs, axr, h_dev)
    g_wait(2)
    combine(0, 1)
    across(0, 0)
    g_wait(3)
    across(0, 1)
    g_wait(4)
    for s in range(2):
        sp = total(0, s)
        out_panel[0, s * 128 : (s + 1) * 128, :] = -sp
        hi, lo = split(sp)
        sphi[s * 128 : (s + 1) * 128, :] = hi
        splo[s * 128 : (s + 1) * 128, :] = lo
    start(1, 0, diag_part)
    start(1, 1, diag_part)
    arrived(xtop, axs, axr, h_dev)
    for i in range(4):
        out_top[i * 128 : (i + 1) * 128, :] = acc[4 * xh + i] + xtop[i]
    combine(1, 0)
    combine(1, 1)
    across(1, 0)
    across(1, 1)
    for s in range(2):
        rows = slice(s * 128, (s + 1) * 128)
        out_diag[0, rows, :] = diag[0, rows, :] + total(1, s)
    for desc in sent:
        desc.wait_send()


def per_device(top_inverse, pattern, panel, diag_inverse):
    vmem = pl.BlockSpec(memory_space=pltpu.VMEM)
    dma = pltpu.SemaphoreType.DMA
    return pl.pallas_call(
        kernel,
        out_shape=(
            jax.ShapeDtypeStruct(top_inverse.shape, F32),
            jax.ShapeDtypeStruct(diag_inverse.shape, F32),
            jax.ShapeDtypeStruct(diag_inverse.shape, F32),
        ),
        in_specs=[pl.BlockSpec(memory_space=pltpu.SMEM), vmem, vmem, vmem],
        out_specs=(vmem, vmem, vmem),
        scratch_shapes=[
            pltpu.VMEM((32, 2, 128, 256), F32),
            pltpu.VMEM((32, 2, 128, 256), BF16),
            pltpu.VMEM((32, 2, 128, 256), BF16),
            pltpu.VMEM((2, 256, 256), BF16),
            pltpu.VMEM((8, 256, 256), F32),
            pltpu.VMEM((8, 256, 256), BF16),
            pltpu.VMEM((8, 256, 256), BF16),
            pltpu.VMEM((2, 256, 256), F32),
            pltpu.VMEM((2, 256, 256), BF16),
            pltpu.VMEM((2, 256, 256), BF16),
            pltpu.VMEM((8, 8, 64, 128), F32),
            pltpu.VMEM((8, 2, 2, 64, 128), F32),
            pltpu.VMEM((8, 2, 64, 128), F32),
            pltpu.VMEM((8, 128, 128), F32),
            pltpu.VMEM((4, 128, 128), F32),
            pltpu.VMEM((2, 2, 8, 128, 256), F32),
            pltpu.VMEM((2, 2, 2, 2, 128, 256), F32),
            pltpu.VMEM((2, 2, 2, 128, 256), F32),
            pltpu.VMEM((2, 2, 128, 256), F32),
            pltpu.VMEM((256, 256), BF16),
            pltpu.VMEM((256, 256), BF16),
            dma((2, 4, 3)), dma((2, 4, 3)), dma((9,)), dma((9,)), dma((8, 4)), dma((8, 4)),
            dma((8, 4)), dma((8, 4)), dma((2, 2, 5)), dma((2, 2, 5)), dma((2, 4)), dma((2, 4)),
            dma, dma,
        ],
        compiler_params=pltpu.CompilerParams(
            collective_id=0, has_side_effects=True, vmem_limit_bytes=60 * 2**20
        ),
    )(pattern, top_inverse, panel, diag_inverse)


def solution(mesh):
    return jax.shard_map(
        per_device,
        mesh=mesh,
        in_specs=(P("row", ("leaf", "col")), P("leaf", None), P("leaf", None, "col"), P("leaf", "row", "col")),
        out_specs=(P("row", ("leaf", "col")), P("leaf", "row", "col"), P("leaf", "row", "col")),
        check_vma=False,
    )
```

```python
import jax
import jax.numpy as jnp
from jax import lax
from jax.experimental import pallas as pl
from jax.experimental.pallas import tpu as pltpu
from jax.sharding import PartitionSpec as P

F32, BF16 = jnp.float32, jnp.bfloat16
NZ, NY = 8, 4


def split(x):
    hi = x.astype(BF16)
    return hi, (x - hi.astype(F32)).astype(BF16)


def mm(a, b):
    return jnp.dot(a, b, preferred_element_type=F32)


def kernel(
    pat, top_hbm, panel_hbm, top_sum, panel_sum, diag_sum,
    top, panel, out_top, out_panel, out_diag, slab, shi, slo, jcat, ptr, pthi, ptlo, xt, xhi, xlo,
    tsl, tr1, tr2, acc, xtop, psl, pr1, pr2, px, vs, vo, vr, v1, v2, sphi, splo,
    loads, *sems,
):
    names = "zxctqvga"
    leaf, row, col = lax.axis_index("leaf"), lax.axis_index("row"), lax.axis_index("col")
    y, xh = row // 2, row % 2
    mod8 = lambda k: (col + k + 16) % 8
    z_dev = ({"col": mod8(1)}, {"col": mod8(-1)})
    y_dev = ({"row": (row + 2) % 8}, {"row": (row + 6) % 8})
    xl = (leaf + 2) % 4
    x_dev = {"leaf": xl}
    lc = leaf + 1 - 2 * (leaf % 2)
    lx = (lc + 2) % 4
    c_dev = {"leaf": lc}
    h_dev = {"row": row + 1 - 2 * xh}

    fetch_top = pltpu.make_async_copy(top_hbm, top, loads.at[0])
    fetch_panel = pltpu.make_async_copy(panel_hbm, panel, loads.at[1])
    fetch_top.start()
    fetch_panel.start()
    sem = pltpu.get_barrier_semaphore()
    peers = (*z_dev, *y_dev, x_dev, c_dev, h_dev)
    for dev in peers:
        pl.semaphore_signal(sem, inc=1, device_id=dev, device_id_type=pl.DeviceIdType.MESH)

    own = leaf * 8 + col
    fetch_top.wait()
    for h in range(2):
        slab[own, h] = top[h * 256 : (h + 1) * 256, :].T
    pl.semaphore_wait(sem, len(peers))

    sent = []

    def copy(src, dst, key, dev):
        k = names.index(key[0])
        return pltpu.make_async_remote_copy(
            src_ref=src, dst_ref=dst, send_sem=sems[2 * k].at[key[1:]], recv_sem=sems[2 * k + 1].at[key[1:]],
            device_id=dev, device_id_type=pl.DeviceIdType.MESH,
        )

    def send(src, dst, key, dev):
        desc = copy(src, dst, key, dev)
        desc.start()
        sent.append(desc)

    def arrived(dst, key, dev):
        copy(dst, dst, key, dev).wait_recv()

    def origin(p):
        return mod8(0 if p == 0 else -p if p < 4 else p - 3 if p < 7 else 4)

    def z_unit(d, t, u, hop):
        o = mod8((hop - t) if d == 0 else (t - hop))
        ref = slab.at[(leaf if u < 2 else xl) * 8 + o, 0 if u == 0 else 1]
        return ref.at[pl.ds(64 * d, 64)] if t == 4 else ref

    def z_send(d, t, u):
        ref = z_unit(d, t, u, 1)
        send(ref, ref, ("z", d, t - 1, u), z_dev[d])

    def z_wait(d, t, u):
        arrived(z_unit(d, t, u, 0), ("z", d, t - 1, u), z_dev[d])

    def x_send(p):
        ref = slab.at[leaf * 8 + origin(p), 0]
        send(ref, ref, ("x", p), x_dev)

    def x_wait(p):
        arrived(slab.at[xl * 8 + origin(p), 0], ("x", p), x_dev)

    halves = ((0, 0), (0, 1), (1, 1), (1, 0))

    def c_send(p, k):
        far, h = halves[k]
        ref = slab.at[(xl if far else leaf) * 8 + origin(p), h]
        send(ref, ref, ("c", p, k), c_dev)

    def c_wait(p):
        for k, (far, h) in enumerate(halves):
            arrived(slab.at[(lx if far else lc) * 8 + origin(p), h], ("c", p, k), c_dev)

    def top_slice(p):
        c_wait(p)
        zz = origin(p)

        def body(rel, _):
            b = ((y + rel) % 4) * 8 + zz
            a0h, a0l = split(slab[b, 0])
            a1h, a1l = split(slab[b, 1])
            shi[b, 0] = a0h
            shi[b, 1] = a1h
            slo[b, 0] = a0l
            slo[b, 1] = a1l
            wide = mm(a0h, jcat[0]) + mm(a1h, jcat[1])
            low = mm(a0l, jcat[0, :, :128]) + mm(a1l, jcat[1, :, :128])
            t = wide[:, :128] + wide[:, 128:] + low
            tsl[p, (2 * rel + 4) % 8] = t[:64]
            tsl[p, (2 * rel + 7) % 8] = t[64:]
            return 0

        lax.fori_loop(0, 4, body, 0)
        for d in range(2):
            send(tsl.at[p, pl.ds(2 * d, 2)], tr1.at[p, d], ("t", p, d), y_dev[d])

    def top_combine(ps):
        for p in ps:
            for d, slot in ((0, 6), (1, 5)):
                arrived(tr1.at[p, d], ("t", p, d), y_dev[d])
                tsl[p, slot] += tr1[p, d, d]
                send(tsl.at[p, slot], tr2.at[p, d], ("t", p, 2 + d), y_dev[d])

    def top_finish(ps):
        for p in ps:
            for d in range(2):
                arrived(tr2.at[p, d], ("t", p, 2 + d), y_dev[d])
            o = origin(p)
            acc[o, :64] = tsl[p, 4] + tr1[p, 1, 0] + tr2[p, 0]
            acc[o, 64:] = tsl[p, 7] + tr1[p, 0, 1] + tr2[p, 1]

    for d in range(2):
        z_send(d, 1, 0)
        z_send(d, 1, 1)
    ref = slab.at[own, 1]
    send(ref, ref, ("x", 8), x_dev)
    x_send(0)
    c_send(0, 0)
    c_send(0, 1)
    for h in range(2):
        j_hi, j_lo = split(top[h * 256 : (h + 1) * 256, :])
        jcat[h, :, :128] = j_hi
        jcat[h, :, 128:] = j_lo
    arrived(slab.at[xl * 8 + col, 1], ("x", 8), x_dev)
    for d in range(2):
        z_send(d, 1, 2)
    c_send(0, 2)

    fetch_panel.wait()

    def turn(i, _):
        block = panel[0, pl.ds(pl.multiple_of(i * 256, 256), 256), :].T
        hi, lo = split(block)
        pthi[i] = hi
        ptlo[i] = lo
        return 0

    lax.fori_loop(0, 8, turn, 0)
    ptr[col] = panel[0, pl.ds(pl.multiple_of(row * 256, 256), 256), :].T
    x_wait(0)
    c_send(0, 3)

    pairs = {0: (0,), 1: (1, 4), 2: (2, 5), 3: (3, 6), 4: (7,)}
    for t in range(1, 5):
        for u in range(3):
            for d in range(2):
                z_wait(d, t, u)
                if t < 4:
                    z_send(d, t + 1, u)
                    if u == 0:
                        x_send(pairs[t][d])
                    c_send(pairs[t][d], u)
            if t == 4:
                if u == 0:
                    x_send(7)
                c_send(7, u)
            if u < len(pairs[t - 1]):
                top_slice(pairs[t - 1][u])
            if u == 1 and t >= 2:
                top_combine(pairs[t - 2])
            if u == 1 and t >= 3:
                top_finish(pairs[t - 3])
        for p in pairs[t]:
            x_wait(p)
            c_send(p, 3)

    def g_unit(d, t, hop):
        ref = ptr.at[mod8((hop - t) if d == 0 else (t - hop))]
        return ref.at[pl.ds(128 * d, 128)] if t == 4 else ref

    def g_send(t):
        for d in range(2):
            ref = g_unit(d, t, 1)
            send(ref, ref, ("g", d, t - 1), z_dev[d])

    def g_wait(t):
        for d in range(2):
            arrived(g_unit(d, t, 0), ("g", d, t - 1), z_dev[d])
        if t < 4:
            g_send(t + 1)

    g_send(1)
    top_combine(pairs[3])
    top_slice(7)
    top_finish(pairs[2])

    for h in range(2):
        xt[h] = jnp.zeros((256, 256), F32)

    def image(i, _):
        b0, b1 = pat[0, 2 * i], pat[0, 2 * i + 1]
        ph, p_lo = pthi[i], ptlo[i]
        for h in range(2):
            bh = jnp.concatenate([shi[b0, h], shi[b1, h]], axis=0)
            bl = jnp.concatenate([slo[b0, h], slo[b1, h]], axis=0)
            xt[h] += mm(ph, bh) + mm(p_lo, bh) + mm(ph, bl)
        return 0

    lax.fori_loop(0, 8, image, 0)
    for h in range(2):
        hi, lo = split(xt[h].T)
        xhi[h] = hi
        xlo[h] = lo
    top_combine(pairs[4])
    top_finish(pairs[3])

    def rel_of(k):
        return ((k + 1) // 2 + 2 * (1 - k % 2)) % 4

    def panel_part(s, rel, ab):
        b = pat[0, 4 * ((y + rel) % 4) + 2 * ab + s]
        total = jnp.zeros((128, 256), F32)
        for h in range(2):
            ah, al = shi[b, h], slo[b, h]
            total += mm(ah, xhi[h]) + mm(ah, xlo[h]) + mm(al, xhi[h])
        return total

    def diag_part(s, rel, ab):
        ah, al = split(ptr[2 * ((y + rel) % 4) + ab, s * 128 : (s + 1) * 128, :])
        return mm(ah, sphi[...]) + mm(ah, splo[...]) + mm(al, sphi[...])

    def start(q, part):
        def far(rel):
            vs[q, rel] = part(1, rel, 1 - xh)
            send(vs.at[q, rel], vr.at[q, rel], ("v", q, rel), h_dev)

        def u_body(k, _):
            psl[q, k] = part(0, rel_of(k), k % 2)
            return 0

        def v_body(rel, _):
            value = part(1, rel, xh)
            vo[q, rel, 0] = value[:64]
            vo[q, rel, 1] = value[64:]
            return 0

        far(2)
        lax.fori_loop(0, 4, u_body, 0)
        for d in range(2):
            send(psl.at[q, pl.ds(2 * d, 2)], pr1.at[q, d], ("q", q, d), y_dev[d])
        for rel in (1, 3, 0):
            far(rel)
        lax.fori_loop(0, 4, v_body, 0)
        lax.fori_loop(4, 8, u_body, 0)

    def v_add(q, rel):
        arrived(vr.at[q, rel], ("v", q, rel), h_dev)
        vo[q, rel, 0] += vr[q, rel, :64]
        vo[q, rel, 1] += vr[q, rel, 64:]

    def v_first(q):
        v_add(q, 2)
        for d in range(2):
            send(vo.at[q, 2, d], v1.at[q, d], ("v", q, 4 + d), y_dev[d])

    def v_second(q):
        for d, rel in ((0, 1), (1, 3)):
            v_add(q, rel)
            arrived(v1.at[q, d], ("v", q, 4 + d), y_dev[d])
            vo[q, rel, d] += v1[q, d]
            send(vo.at[q, rel], v2.at[q, d], ("v", q, 6 + d), y_dev[d])

    def v_total(q):
        v_add(q, 0)
        for d in range(2):
            arrived(v2.at[q, d], ("v", q, 6 + d), y_dev[d])
        return [vo[q, 0, i] + v2[q, 0, i] + v2[q, 1, i] for i in range(2)]

    def u_combine(q):
        for d, slot in ((0, 6), (1, 5)):
            arrived(pr1.at[q, d], ("q", q, d), y_dev[d])
            psl[q, slot] += pr1[q, d, d]
            send(psl.at[q, slot], pr2.at[q, d], ("q", q, 2 + d), y_dev[d])

    def u_across(q):
        for d in range(2):
            arrived(pr2.at[q, d], ("q", q, 2 + d), y_dev[d])
        psl[q, 4] += pr1[q, 1, 0] + pr2[q, 0]
        psl[q, 7] += pr1[q, 0, 1] + pr2[q, 1]
        send(psl.at[q, 7 - 3 * xh], px.at[q], ("q", q, 4), h_dev)

    def u_total(q):
        arrived(px.at[q], ("q", q, 4), h_dev)
        return psl[q, 4 + 3 * xh] + px[q]

    start(0, panel_part)
    v_first(0)
    g_wait(1)
    u_combine(0)
    top_finish(pairs[4])
    v_second(0)
    g_wait(2)
    u_across(0)
    ref = acc.at[pl.ds(4 * (1 - xh), 4)]
    send(ref, xtop, ("a", 0), h_dev)
    g_wait(3)

    def keep(rows, sp):
        out_panel[rows, :] = sp
        hi, lo = split(sp)
        sphi[rows, :] = hi
        splo[rows, :] = lo

    for i, part in enumerate(v_total(0)):
        keep(slice(128 + 64 * i, 192 + 64 * i), part)
    g_wait(4)
    keep(slice(0, 128), u_total(0))
    keep_panel = pltpu.make_async_copy(out_panel, panel_sum, loads.at[2])
    keep_panel.start()
    start(1, diag_part)
    v_first(1)
    arrived(xtop, ("a", 0), h_dev)
    for i in range(4):
        out_top[i * 128 : (i + 1) * 128, :] = acc[4 * xh + i] + xtop[i]
    keep_top = pltpu.make_async_copy(out_top, top_sum, loads.at[3])
    keep_top.start()
    u_combine(1)
    v_second(1)
    u_across(1)
    for i, part in enumerate(v_total(1)):
        out_diag[128 + 64 * i : 192 + 64 * i, :] = part
    out_diag[:128, :] = u_total(1)
    keep_diag = pltpu.make_async_copy(out_diag, diag_sum, loads.at[4])
    keep_diag.start()
    for desc in (keep_panel, keep_top, keep_diag):
        desc.wait()
    for desc in sent:
        desc.wait_send()


def finish(top_in, panel_in, update_in, diag_in, top_out, panel_out, diag_out, top, sp, upd, diag, sems):
    pairs = ((top_in, top), (panel_in, sp), (update_in, upd), (diag_in, diag))
    loads = [pltpu.make_async_copy(a, b, sems.at[i]) for i, (a, b) in enumerate(pairs)]
    for load in loads:
        load.start()
    loads[0].wait()
    stores = [pltpu.make_async_copy(top, top_out, sems.at[4])]
    stores[0].start()
    loads[1].wait()
    sp[...] = -sp[...]
    stores.append(pltpu.make_async_copy(sp, panel_out.at[0], sems.at[5]))
    stores[1].start()
    loads[2].wait()
    loads[3].wait()
    upd[...] = diag[0] + upd[...]
    stores.append(pltpu.make_async_copy(upd, diag_out.at[0], sems.at[6]))
    stores[2].start()
    for store in stores:
        store.wait()


def per_device(top_inverse, pattern, panel, diag_inverse):
    hbm = pl.BlockSpec(memory_space=pl.ANY)
    smem = pl.BlockSpec(memory_space=pltpu.SMEM)
    dma, f32, b16 = pltpu.SemaphoreType.DMA, lambda *n: pltpu.VMEM(n, F32), lambda *n: pltpu.VMEM(n, BF16)
    shape = lambda *n: jax.ShapeDtypeStruct(n, F32)
    counts = ((2, 4, 3), (9,), (8, 4), (8, 4), (2, 5), (2, 8), (2, 4), (1,))
    sums = pl.pallas_call(
        kernel,
        out_shape=(shape(512, 128), shape(256, 256), shape(256, 256)),
        in_specs=[smem, hbm, hbm],
        out_specs=(hbm, hbm, hbm),
        scratch_shapes=[
            f32(512, 128), f32(1, 2048, 256), f32(512, 128), f32(256, 256), f32(256, 256),
            f32(32, 2, 128, 256), b16(32, 2, 128, 256), b16(32, 2, 128, 256),
            b16(2, 256, 256), f32(8, 256, 256), b16(8, 256, 256), b16(8, 256, 256),
            f32(2, 256, 256), b16(2, 256, 256), b16(2, 256, 256),
            f32(8, 8, 64, 128), f32(8, 2, 2, 64, 128), f32(8, 2, 64, 128),
            f32(8, 128, 128), f32(4, 128, 128),
            f32(2, 8, 128, 256), f32(2, 2, 2, 128, 256), f32(2, 2, 128, 256), f32(2, 128, 256),
            f32(2, 4, 128, 256), f32(2, 4, 2, 64, 256), f32(2, 4, 128, 256),
            f32(2, 2, 64, 256), f32(2, 2, 2, 64, 256),
            b16(256, 256), b16(256, 256),
            dma((5,)), *(dma(n) for n in counts for _ in range(2)),
        ],
        compiler_params=pltpu.CompilerParams(
            collective_id=0, has_side_effects=True, vmem_limit_bytes=60 * 2**20
        ),
    )(pattern, top_inverse, panel)
    return pl.pallas_call(
        finish,
        out_shape=(shape(512, 128), shape(1, 256, 256), shape(1, 256, 256)),
        in_specs=[hbm] * 4,
        out_specs=(hbm, hbm, hbm),
        scratch_shapes=[f32(512, 128), f32(256, 256), f32(256, 256), f32(1, 256, 256), dma((7,))],
    )(*sums, diag_inverse)


def solution(mesh):
    return jax.shard_map(
        per_device,
        mesh=mesh,
        in_specs=(P("row", ("leaf", "col")), P("leaf", None), P("leaf", None, "col"), P("leaf", "row", "col")),
        out_specs=(P("row", ("leaf", "col")), P("leaf", "row", "col"), P("leaf", "row", "col")),
        check_vma=False,
    )
```

```python
import jax
import jax.numpy as jnp
from jax import lax
from jax.experimental import pallas as pl
from jax.experimental.pallas import tpu as pltpu
from jax.sharding import PartitionSpec as P

F32, BF16 = jnp.float32, jnp.bfloat16
NZ, NY = 8, 4


def split(x):
    hi = x.astype(BF16)
    return hi, (x - hi.astype(F32)).astype(BF16)


def mm(a, b):
    return jnp.dot(a, b, preferred_element_type=F32)


def kernel(
    pat, top_hbm, panel_hbm, top_sum, panel_sum, diag_sum,
    kept, given, panel, out_top, out_panel, out_diag, slab, shi, slo, jcat, ptr, pthi, ptlo, xt, xhi, xlo,
    tsl, tr1, tr2, acc, xtop, psl, pr1, pr2, px, vs, vo, vr, v1, v2, sphi, splo,
    loads, *sems,
):
    names = "zxctqvgaw"
    leaf, row, col = lax.axis_index("leaf"), lax.axis_index("row"), lax.axis_index("col")
    y, xh = row // 2, row % 2
    mod8 = lambda k: (col + k + 16) % 8
    z_dev = ({"col": mod8(1)}, {"col": mod8(-1)})
    y_dev = ({"row": (row + 2) % 8}, {"row": (row + 6) % 8})
    xl = (leaf + 2) % 4
    x_dev = {"leaf": xl}
    lc = leaf + 1 - 2 * (leaf % 2)
    lx = (lc + 2) % 4
    c_dev = {"leaf": lc}
    h_dev = {"row": row + 1 - 2 * xh}

    light = 1 - y // 2
    mate = (3 - y) * 2 + xh
    low, high = row * light + mate * (1 - light), row * (1 - light) + mate * light
    l0 = leaf % 2

    def has(b, h):
        return b // 4 <= (low if h else high)

    fetch_kept = pltpu.make_async_copy(top_hbm.at[pl.ds(0, 256)], kept.at[light], loads.at[0])
    fetch_given = pltpu.make_async_copy(top_hbm.at[pl.ds(256, 256)], given, loads.at[5])
    fetch_panel = pltpu.make_async_copy(panel_hbm, panel, loads.at[1])
    fetch_kept.start()
    fetch_given.start()
    fetch_panel.start()
    sem = pltpu.get_barrier_semaphore()
    peers = (*z_dev, *y_dev, x_dev, c_dev, h_dev)
    for dev in peers:
        pl.semaphore_signal(sem, inc=1, device_id=dev, device_id_type=pl.DeviceIdType.MESH)

    zeros = jnp.zeros((128, 256), F32)

    def clear(i, _):
        slab[16 + i, 1] = zeros
        return 0

    def clear_own(o, _):
        for b, h in ((leaf * 8 + o, 0), (xl * 8 + o, 0), (l0 * 8 + o, 1)):

            @pl.when(jnp.logical_not(has(b, h)))
            def _():
                slab[b, h] = zeros

        return 0

    lax.fori_loop(0, 16, clear, 0)
    lax.fori_loop(0, 8, clear_own, 0)

    own = leaf * 8 + col
    fetch_kept.wait()
    slab[own, light] = kept[light].T
    fetch_given.wait()
    pl.semaphore_wait(sem, len(peers))

    sent = []

    def copy(src, dst, key, dev):
        k = names.index(key[0])
        return pltpu.make_async_remote_copy(
            src_ref=src, dst_ref=dst, send_sem=sems[2 * k].at[key[1:]], recv_sem=sems[2 * k + 1].at[key[1:]],
            device_id=dev, device_id_type=pl.DeviceIdType.MESH,
        )

    def send(src, dst, key, dev, cond=None):
        desc = copy(src, dst, key, dev)
        if cond is None:
            desc.start()
        else:
            pl.when(cond)(desc.start)
        sent.append((desc, cond))

    def arrived(dst, key, dev, cond=None):
        desc = copy(dst, dst, key, dev)
        if cond is None:
            desc.wait_recv()
        else:
            pl.when(cond)(desc.wait_recv)

    def origin(p):
        return mod8(0 if p == 0 else -p if p < 4 else p - 3 if p < 7 else 4)

    def z_unit(d, t, u, hop):
        o = mod8((hop - t) if d == 0 else (t - hop))
        b = (leaf, leaf, xl, l0)[u] * 8 + o
        first, rows = ((0, 64), (64, 64), (64, 64), (0, 128))[u]
        if t == 4:
            first, rows = first + rows // 2 * d, rows // 2
        return slab.at[b, u // 3, pl.ds(first, rows)], has(b, u // 3)

    def z_send(d, t, u):
        ref, cond = z_unit(d, t, u, 1)
        send(ref, ref, ("z", d, t - 1, u), z_dev[d], cond)

    def z_wait(d, t, u):
        ref, cond = z_unit(d, t, u, 0)
        arrived(ref, ("z", d, t - 1, u), z_dev[d], cond)

    def x_send(p):
        b = leaf * 8 + origin(p)
        ref = slab.at[b, 0, pl.ds(0, 64)]
        send(ref, ref, ("x", p), x_dev, has(b, 0))

    def x_wait(p):
        b = xl * 8 + origin(p)
        arrived(slab.at[b, 0, pl.ds(0, 64)], ("x", p), x_dev, has(b, 0))

    def c_send(p, k):
        ref = slab.at[(leaf, xl, l0)[k] * 8 + origin(p), k // 2]
        send(ref, ref, ("c", p, k), c_dev)

    def c_wait(p):
        for k in range(3):
            arrived(slab.at[(lc, lx, 1 - l0)[k] * 8 + origin(p), k // 2], ("c", p, k), c_dev)

    def top_slice(p):
        c_wait(p)
        zz = origin(p)

        def body(rel, _):
            b = ((y + rel) % 4) * 8 + zz
            a0h, a0l = split(slab[b, 0])
            a1h, a1l = split(slab[b, 1])
            shi[b, 0] = a0h
            shi[b, 1] = a1h
            slo[b, 0] = a0l
            slo[b, 1] = a1l
            wide = mm(a0h, jcat[0]) + mm(a1h, jcat[1])
            low = mm(a0l, jcat[0, :, :128]) + mm(a1l, jcat[1, :, :128])
            t = wide[:, :128] + wide[:, 128:] + low
            tsl[p, (2 * rel + 4) % 8] = t[:64]
            tsl[p, (2 * rel + 7) % 8] = t[64:]
            return 0

        lax.fori_loop(0, 4, body, 0)
        for d in range(2):
            send(tsl.at[p, pl.ds(2 * d, 2)], tr1.at[p, d], ("t", p, d), y_dev[d])

    def top_combine(ps):
        for p in ps:
            for d, slot in ((0, 6), (1, 5)):
                arrived(tr1.at[p, d], ("t", p, d), y_dev[d])
                tsl[p, slot] += tr1[p, d, d]
                send(tsl.at[p, slot], tr2.at[p, d], ("t", p, 2 + d), y_dev[d])

    def top_finish(ps):
        for p in ps:
            for d in range(2):
                arrived(tr2.at[p, d], ("t", p, 2 + d), y_dev[d])
            o = origin(p)
            acc[o, :64] = tsl[p, 4] + tr1[p, 1, 0] + tr2[p, 0]
            acc[o, 64:] = tsl[p, 7] + tr1[p, 0, 1] + tr2[p, 1]

    send(given, kept.at[light], ("w", 0), {"row": mate})
    ref_b, ref_l = slab.at[own, 0, pl.ds(64, 64)], slab.at[l0 * 8 + col, 1]
    near = leaf // 2 == 0
    low_here = has(l0 * 8 + col, 1)

    def start_high():
        for d in range(2):
            for u in range(2):
                z_send(d, 1, u)
        send(ref_b, ref_b, ("x", 8), x_dev, has(own, 0))
        x_send(0)
        c_send(0, 0)

    def start_low():
        for d in range(2):
            z_send(d, 1, 3)
        send(ref_l, ref_l, ("x", 9), x_dev, low_here)
        c_send(0, 2)

    mark = len(sent)
    pl.when(light == 0)(start_high)
    pl.when(jnp.logical_and(light == 1, near))(start_low)
    del sent[mark:]
    arrived(kept.at[1 - light], ("w", 0), {"row": mate})
    slab[own, 1 - light] = kept[1 - light].T
    pl.when(light == 1)(start_high)
    pl.when(jnp.logical_and(light == 0, near))(start_low)
    del sent[mark:]
    for h in range(2):
        j_hi, j_lo = split(kept[h])
        jcat[h, :, :128] = j_hi
        jcat[h, :, 128:] = j_lo
    arrived(slab.at[xl * 8 + col, 0, pl.ds(64, 64)], ("x", 8), x_dev, has(xl * 8 + col, 0))
    for d in range(2):
        z_send(d, 1, 2)

    def pass_low():
        arrived(ref_l, ("x", 9), x_dev, low_here)
        for d in range(2):
            z_send(d, 1, 3)
        c_send(0, 2)

    mark = len(sent)
    pl.when(leaf // 2 == 1)(pass_low)
    del sent[mark:]
    for d in range(2):
        for u in (0, 1, 3):
            ref, cond = z_unit(d, 1, u, 1)
            sent.append((copy(ref, ref, ("z", d, 0, u), z_dev[d]), cond))
    sent.append((copy(ref_b, ref_b, ("x", 8), x_dev), has(own, 0)))
    ref = slab.at[own, 0, pl.ds(0, 64)]
    sent.append((copy(ref, ref, ("x", 0), x_dev), has(own, 0)))
    sent.append((copy(ref_l, ref_l, ("x", 9), x_dev), jnp.logical_and(low_here, near)))
    for k, ref in ((0, slab.at[own, 0]), (2, ref_l)):
        sent.append((copy(ref, ref, ("c", 0, k), c_dev), None))

    fetch_panel.wait()

    def turn(i, _):
        block = panel[0, pl.ds(pl.multiple_of(i * 256, 256), 256), :].T
        hi, lo = split(block)
        pthi[i] = hi
        ptlo[i] = lo
        return 0

    lax.fori_loop(0, 8, turn, 0)
    ptr[col] = panel[0, pl.ds(pl.multiple_of(row * 256, 256), 256), :].T
    x_wait(0)
    c_send(0, 1)

    def g_units(t, hop):
        for w in range(2):
            for d in range(2):
                if t < 4 or w == d:
                    o = mod8((hop - t) if d == 0 else (t - hop))
                    yield ptr.at[o, pl.ds(128 * w, 128)], ("g", d, t - 1, w), z_dev[d]

    def g_send(t):
        for ref, key, dev in g_units(t, 1):
            send(ref, ref, key, dev)

    def g_wait(t):
        onward = list(g_units(t + 1, 1)) if t < 3 else list(g_units(4, 1)) if t == 3 else []
        for ref, key, dev in g_units(t, 0):
            arrived(ref, key, dev)
            for out, out_key, out_dev in onward:
                if out_key[1] == key[1] and out_key[3] == key[3]:
                    send(out, out, out_key, out_dev)

    pairs = {0: (0,), 1: (1, 4), 2: (2, 5), 3: (3, 6), 4: (7,)}
    for t in range(1, 5):
        for u in range(4):
            for d in range(2):
                z_wait(d, t, u)
                if t < 4:
                    z_send(d, t + 1, u)
            for p in pairs[t]:
                if u == 0:
                    x_send(p)
                if u % 2:
                    c_send(p, u - 1)
            if u < len(pairs[t - 1]):
                top_slice(pairs[t - 1][u])
            if u == 1 and t >= 2:
                top_combine(pairs[t - 2])
            if u == 1 and t >= 3:
                top_finish(pairs[t - 3])
        for p in pairs[t]:
            x_wait(p)
            c_send(p, 1)
        if t == 3:
            g_send(1)

    top_slice(7)
    g_wait(1)

    for h in range(2):
        xt[h] = jnp.zeros((256, 256), F32)

    def image(i, _):
        b0, b1 = pat[0, 2 * i], pat[0, 2 * i + 1]
        ph, p_lo = pthi[i], ptlo[i]
        for h in range(2):
            bh = jnp.concatenate([shi[b0, h], shi[b1, h]], axis=0)
            bl = jnp.concatenate([slo[b0, h], slo[b1, h]], axis=0)
            xt[h] += mm(ph, bh) + mm(p_lo, bh) + mm(ph, bl)
        return 0

    lax.fori_loop(0, 8, image, 0)
    for h in range(2):
        hi, lo = split(xt[h].T)
        xhi[h] = hi
        xlo[h] = lo
    def rel_of(k):
        return ((k + 1) // 2 + 2 * (1 - k % 2)) % 4

    def panel_part(s, rel, ab):
        b = pat[0, 4 * ((y + rel) % 4) + 2 * ab + s]
        total = jnp.zeros((128, 256), F32)
        for h in range(2):
            ah, al = shi[b, h], slo[b, h]
            total += mm(ah, xhi[h]) + mm(ah, xlo[h]) + mm(al, xhi[h])
        return total

    def diag_part(s, rel, ab):
        ah, al = split(ptr[2 * ((y + rel) % 4) + ab, s * 128 : (s + 1) * 128, :])
        return mm(ah, sphi[...]) + mm(ah, splo[...]) + mm(al, sphi[...])

    def start(q, part):
        def far(rel):
            vs[q, rel] = part(1, rel, 1 - xh)
            send(vs.at[q, rel], vr.at[q, rel], ("v", q, rel), h_dev)

        def u_body(k, _):
            psl[q, k] = part(0, rel_of(k), k % 2)
            return 0

        def v_body(rel, _):
            value = part(1, rel, xh)
            vo[q, rel, 0] = value[:64]
            vo[q, rel, 1] = value[64:]
            return 0

        far(2)
        lax.fori_loop(0, 4, u_body, 0)
        for d in range(2):
            send(psl.at[q, pl.ds(2 * d, 2)], pr1.at[q, d], ("q", q, d), y_dev[d])
        for rel in (1, 3, 0):
            far(rel)
        lax.fori_loop(0, 4, v_body, 0)
        lax.fori_loop(4, 8, u_body, 0)

    def v_add(q, rel):
        arrived(vr.at[q, rel], ("v", q, rel), h_dev)
        vo[q, rel, 0] += vr[q, rel, :64]
        vo[q, rel, 1] += vr[q, rel, 64:]

    def v_first(q):
        v_add(q, 2)
        for d in range(2):
            send(vo.at[q, 2, d], v1.at[q, d], ("v", q, 4 + d), y_dev[d])

    def v_second(q):
        for d, rel in ((0, 1), (1, 3)):
            v_add(q, rel)
            arrived(v1.at[q, d], ("v", q, 4 + d), y_dev[d])
            vo[q, rel, d] += v1[q, d]
            send(vo.at[q, rel], v2.at[q, d], ("v", q, 6 + d), y_dev[d])

    def v_total(q):
        v_add(q, 0)
        for d in range(2):
            arrived(v2.at[q, d], ("v", q, 6 + d), y_dev[d])
        return [vo[q, 0, i] + v2[q, 0, i] + v2[q, 1, i] for i in range(2)]

    def u_combine(q):
        for d, slot in ((0, 6), (1, 5)):
            arrived(pr1.at[q, d], ("q", q, d), y_dev[d])
            psl[q, slot] += pr1[q, d, d]
            send(psl.at[q, slot], pr2.at[q, d], ("q", q, 2 + d), y_dev[d])

    def u_across(q):
        for d in range(2):
            arrived(pr2.at[q, d], ("q", q, 2 + d), y_dev[d])
        psl[q, 4] += pr1[q, 1, 0] + pr2[q, 0]
        psl[q, 7] += pr1[q, 0, 1] + pr2[q, 1]
        send(psl.at[q, 7 - 3 * xh], px.at[q], ("q", q, 4), h_dev)

    def u_total(q):
        arrived(px.at[q], ("q", q, 4), h_dev)
        return psl[q, 4 + 3 * xh] + px[q]

    start(0, panel_part)
    g_wait(2)
    top_combine(pairs[3])
    v_first(0)
    top_finish(pairs[2])
    top_combine(pairs[4])
    u_combine(0)
    g_wait(3)
    v_second(0)
    u_across(0)
    top_finish(pairs[3])
    top_finish(pairs[4])
    ref = acc.at[pl.ds(4 * (1 - xh), 4)]
    send(ref, xtop, ("a", 0), h_dev)

    def keep(rows, sp):
        out_panel[rows, :] = sp
        hi, lo = split(sp)
        sphi[rows, :] = hi
        splo[rows, :] = lo

    for i, part in enumerate(v_total(0)):
        keep(slice(128 + 64 * i, 192 + 64 * i), part)
    g_wait(4)
    keep(slice(0, 128), u_total(0))
    keep_panel = pltpu.make_async_copy(out_panel, panel_sum, loads.at[2])
    keep_panel.start()
    start(1, diag_part)
    v_first(1)
    arrived(xtop, ("a", 0), h_dev)
    for i in range(4):
        out_top[i * 128 : (i + 1) * 128, :] = acc[4 * xh + i] + xtop[i]
    keep_top = pltpu.make_async_copy(out_top, top_sum, loads.at[3])
    keep_top.start()
    u_combine(1)
    v_second(1)
    u_across(1)
    for i, part in enumerate(v_total(1)):
        out_diag[128 + 64 * i : 192 + 64 * i, :] = part
    out_diag[:128, :] = u_total(1)
    keep_diag = pltpu.make_async_copy(out_diag, diag_sum, loads.at[4])
    keep_diag.start()
    for desc in (keep_panel, keep_top, keep_diag):
        desc.wait()
    for desc, cond in sent:
        if cond is None:
            desc.wait_send()
        else:
            pl.when(cond)(desc.wait_send)


def finish(top_in, panel_in, update_in, diag_in, top_out, panel_out, diag_out, top, sp, upd, diag, sems):
    pairs = ((top_in, top), (panel_in, sp), (update_in, upd), (diag_in, diag))
    loads = [pltpu.make_async_copy(a, b, sems.at[i]) for i, (a, b) in enumerate(pairs)]
    for load in loads:
        load.start()
    loads[0].wait()
    stores = [pltpu.make_async_copy(top, top_out, sems.at[4])]
    stores[0].start()
    loads[1].wait()
    sp[...] = -sp[...]
    stores.append(pltpu.make_async_copy(sp, panel_out.at[0], sems.at[5]))
    stores[1].start()
    loads[2].wait()
    loads[3].wait()
    upd[...] = diag[0] + upd[...]
    stores.append(pltpu.make_async_copy(upd, diag_out.at[0], sems.at[6]))
    stores[2].start()
    for store in stores:
        store.wait()


def per_device(top_inverse, pattern, panel, diag_inverse):
    hbm = pl.BlockSpec(memory_space=pl.ANY)
    smem = pl.BlockSpec(memory_space=pltpu.SMEM)
    dma, f32, b16 = pltpu.SemaphoreType.DMA, lambda *n: pltpu.VMEM(n, F32), lambda *n: pltpu.VMEM(n, BF16)
    shape = lambda *n: jax.ShapeDtypeStruct(n, F32)
    counts = ((2, 4, 4), (10,), (8, 3), (8, 4), (2, 5), (2, 8), (2, 4, 2), (1,), (1,))
    sums = pl.pallas_call(
        kernel,
        out_shape=(shape(512, 128), shape(256, 256), shape(256, 256)),
        in_specs=[smem, hbm, hbm],
        out_specs=(hbm, hbm, hbm),
        scratch_shapes=[
            f32(2, 256, 128), f32(256, 128), f32(1, 2048, 256), f32(512, 128), f32(256, 256), f32(256, 256),
            f32(32, 2, 128, 256), b16(32, 2, 128, 256), b16(32, 2, 128, 256),
            b16(2, 256, 256), f32(8, 256, 256), b16(8, 256, 256), b16(8, 256, 256),
            f32(2, 256, 256), b16(2, 256, 256), b16(2, 256, 256),
            f32(8, 8, 64, 128), f32(8, 2, 2, 64, 128), f32(8, 2, 64, 128),
            f32(8, 128, 128), f32(4, 128, 128),
            f32(2, 8, 128, 256), f32(2, 2, 2, 128, 256), f32(2, 2, 128, 256), f32(2, 128, 256),
            f32(2, 4, 128, 256), f32(2, 4, 2, 64, 256), f32(2, 4, 128, 256),
            f32(2, 2, 64, 256), f32(2, 2, 2, 64, 256),
            b16(256, 256), b16(256, 256),
            dma((6,)), *(dma(n) for n in counts for _ in range(2)),
        ],
        compiler_params=pltpu.CompilerParams(
            collective_id=0, has_side_effects=True, vmem_limit_bytes=60 * 2**20
        ),
    )(pattern, top_inverse, panel)
    return pl.pallas_call(
        finish,
        out_shape=(shape(512, 128), shape(1, 256, 256), shape(1, 256, 256)),
        in_specs=[hbm] * 4,
        out_specs=(hbm, hbm, hbm),
        scratch_shapes=[f32(512, 128), f32(256, 256), f32(256, 256), f32(1, 256, 256), dma((7,))],
    )(*sums, diag_inverse)


def solution(mesh):
    return jax.shard_map(
        per_device,
        mesh=mesh,
        in_specs=(P("row", ("leaf", "col")), P("leaf", None), P("leaf", None, "col"), P("leaf", "row", "col")),
        out_specs=(P("row", ("leaf", "col")), P("leaf", "row", "col"), P("leaf", "row", "col")),
        check_vma=False,
    )
```

```python
import jax
import jax.numpy as jnp
from jax import lax
from jax.experimental import pallas as pl
from jax.experimental.pallas import tpu as pltpu
from jax.sharding import PartitionSpec as P

F32, BF16 = jnp.float32, jnp.bfloat16
NZ, NY = 8, 4


def split(x):
    hi = x.astype(BF16)
    return hi, (x - hi.astype(F32)).astype(BF16)


def mm(a, b):
    return jnp.dot(a, b, preferred_element_type=F32)


def kernel(
    pat, top_hbm, panel_hbm, top_sum, panel_sum, diag_sum,
    kept, given, panel, out_top, out_panel, out_diag, slab, shi, slo, jcat, ptr, pt, xt, xhi, xlo,
    tsl, tr1, tr2, acc, xtop, psl, pr1, pr2, px, vs, vo, vr, v1, v2, sphi, splo,
    loads, *sems,
):
    names = "zxctqvgaw"
    leaf, row, col = lax.axis_index("leaf"), lax.axis_index("row"), lax.axis_index("col")
    y, xh = row // 2, row % 2
    mod8 = lambda k: (col + k + 16) % 8
    z_dev = ({"col": mod8(1)}, {"col": mod8(-1)})
    y_dev = ({"row": (row + 2) % 8}, {"row": (row + 6) % 8})
    xl = (leaf + 2) % 4
    x_dev = {"leaf": xl}
    lc = leaf + 1 - 2 * (leaf % 2)
    lx = (lc + 2) % 4
    c_dev = {"leaf": lc}
    h_dev = {"row": row + 1 - 2 * xh}

    light = 1 - y // 2
    mate = (3 - y) * 2 + xh
    low, high = row * light + mate * (1 - light), row * (1 - light) + mate * light
    l0 = leaf % 2

    def has(b, h):
        return b // 4 <= (low if h else high)

    fetch_kept = pltpu.make_async_copy(top_hbm.at[pl.ds(0, 256)], kept.at[light], loads.at[0])
    fetch_given = pltpu.make_async_copy(top_hbm.at[pl.ds(256, 256)], given, loads.at[5])
    fetch_panel = pltpu.make_async_copy(panel_hbm, panel, loads.at[1])
    fetch_kept.start()
    fetch_given.start()
    fetch_panel.start()
    sem = pltpu.get_barrier_semaphore()
    peers = (*z_dev, *y_dev, x_dev, c_dev, h_dev)
    for dev in peers:
        pl.semaphore_signal(sem, inc=1, device_id=dev, device_id_type=pl.DeviceIdType.MESH)

    zeros = jnp.zeros((128, 256), F32)

    def clear(i, _):
        shi[16 + i, 1] = zeros.astype(BF16)
        slo[16 + i, 1] = zeros.astype(BF16)
        return 0

    def clear_own(o, _):
        for b, h in ((leaf * 8 + o, 0), (xl * 8 + o, 0), (l0 * 8 + o, 1)):

            @pl.when(jnp.logical_not(has(b, h)))
            def _():
                slab[b, h] = zeros

        return 0

    lax.fori_loop(0, 16, clear, 0)
    lax.fori_loop(0, 8, clear_own, 0)

    own = leaf * 8 + col
    fetch_kept.wait()
    slab[own, light] = kept[light].T
    fetch_given.wait()
    pl.semaphore_wait(sem, len(peers))

    sent = []

    def copy(src, dst, key, dev):
        k = names.index(key[0])
        return pltpu.make_async_remote_copy(
            src_ref=src, dst_ref=dst, send_sem=sems[2 * k].at[key[1:]], recv_sem=sems[2 * k + 1].at[key[1:]],
            device_id=dev, device_id_type=pl.DeviceIdType.MESH,
        )

    def send(src, dst, key, dev, cond=None):
        desc = copy(src, dst, key, dev)
        if cond is None:
            desc.start()
        else:
            pl.when(cond)(desc.start)
        sent.append((desc, cond))

    def arrived(dst, key, dev, cond=None):
        desc = copy(dst, dst, key, dev)
        if cond is None:
            desc.wait_recv()
        else:
            pl.when(cond)(desc.wait_recv)

    def origin(p):
        return mod8(0 if p == 0 else -p if p < 4 else p - 3 if p < 7 else 4)

    def z_unit(d, t, u, hop):
        o = mod8((hop - t) if d == 0 else (t - hop))
        b = (leaf, leaf, xl, l0)[u] * 8 + o
        first, rows = ((0, 64), (64, 64), (64, 64), (0, 128))[u]
        if t == 4:
            first, rows = first + rows // 2 * d, rows // 2
        return slab.at[b, u // 3, pl.ds(first, rows)], has(b, u // 3)

    def z_send(d, t, u):
        ref, cond = z_unit(d, t, u, 1)
        send(ref, ref, ("z", d, t - 1, u), z_dev[d], cond)

    def z_wait(d, t, u):
        ref, cond = z_unit(d, t, u, 0)
        arrived(ref, ("z", d, t - 1, u), z_dev[d], cond)

    def x_send(p):
        b = leaf * 8 + origin(p)
        ref = slab.at[b, 0, pl.ds(0, 64)]
        send(ref, ref, ("x", p), x_dev, has(b, 0))

    def x_wait(p):
        b = xl * 8 + origin(p)
        arrived(slab.at[b, 0, pl.ds(0, 64)], ("x", p), x_dev, has(b, 0))

    def c_send(p, k):
        ref = slab.at[(leaf, xl, l0)[k] * 8 + origin(p), k // 2]
        send(ref, ref, ("c", p, k), c_dev)

    def c_wait(p):
        for k in range(3):
            arrived(slab.at[(lc, lx, 1 - l0)[k] * 8 + origin(p), k // 2], ("c", p, k), c_dev)

    def top_slice(p):
        c_wait(p)
        zz = origin(p)
        parts = []
        for h, count in ((0, 4), (1, 2)):
            his, los = [], []
            for far in range(count):
                b = far * 8 + zz
                hi, lo = split(slab[b, h])
                shi[b, h] = hi
                slo[b, h] = lo
                his.append(hi)
                los.append(lo)
            wide = mm(jnp.concatenate(his, axis=0), jcat[h])
            parts.append(wide[:, :128] + wide[:, 128:] + mm(jnp.concatenate(los, axis=0), jcat[h, :, :128]))
        for far in range(4):
            rows = slice(far * 128, (far + 1) * 128)
            t = parts[0][rows] + parts[1][rows] if far < 2 else parts[0][rows]
            rel = (far - y + 4) % 4
            tsl[p, (2 * rel + 4) % 8] = t[:64]
            tsl[p, (2 * rel + 7) % 8] = t[64:]
        for d in range(2):
            send(tsl.at[p, pl.ds(2 * d, 2)], tr1.at[p, d], ("t", p, d), y_dev[d])

    def top_combine(ps):
        for p in ps:
            for d, slot in ((0, 6), (1, 5)):
                arrived(tr1.at[p, d], ("t", p, d), y_dev[d])
                tsl[p, slot] += tr1[p, d, d]
                send(tsl.at[p, slot], tr2.at[p, d], ("t", p, 2 + d), y_dev[d])

    def top_finish(ps):
        for p in ps:
            for d in range(2):
                arrived(tr2.at[p, d], ("t", p, 2 + d), y_dev[d])
            o = origin(p)
            acc[o, :64] = tsl[p, 4] + tr1[p, 1, 0] + tr2[p, 0]
            acc[o, 64:] = tsl[p, 7] + tr1[p, 0, 1] + tr2[p, 1]
            send(acc.at[o], xtop.at[o % 4], ("a", p), h_dev, o // 4 != xh)

    send(given, kept.at[light], ("w", 0), {"row": mate})
    ref_b, ref_l = slab.at[own, 0, pl.ds(64, 64)], slab.at[l0 * 8 + col, 1]
    near = leaf // 2 == 0
    low_here = has(l0 * 8 + col, 1)

    def start_high():
        for d in range(2):
            for u in range(2):
                z_send(d, 1, u)
        send(ref_b, ref_b, ("x", 8), x_dev, has(own, 0))
        x_send(0)
        c_send(0, 0)

    def start_low():
        for d in range(2):
            z_send(d, 1, 3)
        send(ref_l, ref_l, ("x", 9), x_dev, low_here)
        c_send(0, 2)

    mark = len(sent)
    pl.when(light == 0)(start_high)
    pl.when(jnp.logical_and(light == 1, near))(start_low)
    del sent[mark:]
    arrived(kept.at[1 - light], ("w", 0), {"row": mate})
    slab[own, 1 - light] = kept[1 - light].T
    pl.when(light == 1)(start_high)
    pl.when(jnp.logical_and(light == 0, near))(start_low)
    del sent[mark:]
    for h in range(2):
        j_hi, j_lo = split(kept[h])
        jcat[h, :, :128] = j_hi
        jcat[h, :, 128:] = j_lo
    arrived(slab.at[xl * 8 + col, 0, pl.ds(64, 64)], ("x", 8), x_dev, has(xl * 8 + col, 0))
    for d in range(2):
        z_send(d, 1, 2)

    def pass_low():
        arrived(ref_l, ("x", 9), x_dev, low_here)
        for d in range(2):
            z_send(d, 1, 3)
        c_send(0, 2)

    mark = len(sent)
    pl.when(leaf // 2 == 1)(pass_low)
    del sent[mark:]
    for d in range(2):
        for u in (0, 1, 3):
            ref, cond = z_unit(d, 1, u, 1)
            sent.append((copy(ref, ref, ("z", d, 0, u), z_dev[d]), cond))
    sent.append((copy(ref_b, ref_b, ("x", 8), x_dev), has(own, 0)))
    ref = slab.at[own, 0, pl.ds(0, 64)]
    sent.append((copy(ref, ref, ("x", 0), x_dev), has(own, 0)))
    sent.append((copy(ref_l, ref_l, ("x", 9), x_dev), jnp.logical_and(low_here, near)))
    for k, ref in ((0, slab.at[own, 0]), (2, ref_l)):
        sent.append((copy(ref, ref, ("c", 0, k), c_dev), None))

    fetch_panel.wait()

    def turn(i, _):
        block = panel[0, pl.ds(pl.multiple_of(i * 256, 256), 256), :].T
        hi, lo = split(block)
        pt[i, :256] = hi
        pt[i, 256:] = lo
        return 0

    lax.fori_loop(0, 8, turn, 0)
    ptr[col] = panel[0, pl.ds(pl.multiple_of(row * 256, 256), 256), :].T
    x_wait(0)
    c_send(0, 1)

    def g_units(t, hop):
        for w in range(2):
            for d in range(2):
                if t < 4 or w == d:
                    o = mod8((hop - t) if d == 0 else (t - hop))
                    yield ptr.at[o, pl.ds(128 * w, 128)], ("g", d, t - 1, w), z_dev[d]

    def g_send(t):
        for ref, key, dev in g_units(t, 1):
            send(ref, ref, key, dev)

    def g_wait(t):
        onward = list(g_units(t + 1, 1)) if t < 3 else list(g_units(4, 1)) if t == 3 else []
        for ref, key, dev in g_units(t, 0):
            arrived(ref, key, dev)
            for out, out_key, out_dev in onward:
                if out_key[1] == key[1] and out_key[3] == key[3]:
                    send(out, out, out_key, out_dev)

    pairs = {0: (0,), 1: (1, 4), 2: (2, 5), 3: (3, 6), 4: (7,)}
    for t in range(1, 5):
        for u in range(4):
            for d in range(2):
                z_wait(d, t, u)
                if t < 4:
                    z_send(d, t + 1, u)
            for p in pairs[t]:
                if u == 0:
                    x_send(p)
                if u % 2:
                    c_send(p, u - 1)
            for i, p in enumerate(pairs[t - 1]):
                if u == (1, 2)[i]:
                    top_slice(p)
            if u == 3 and t >= 2:
                top_combine(pairs[t - 2])
            if u == 3 and t >= 3:
                top_finish(pairs[t - 3])
        for p in pairs[t]:
            x_wait(p)
            c_send(p, 1)
        if t == 3:
            g_send(1)

    top_slice(7)

    for h in range(2):
        xt[h] = jnp.zeros((256, 256), F32)

    def image(i, _):
        b0, b1 = pat[0, 2 * i], pat[0, 2 * i + 1]
        both = pt[i]
        for h in range(2):
            bh = jnp.concatenate([shi[b0, h], shi[b1, h]], axis=0)
            bl = jnp.concatenate([slo[b0, h], slo[b1, h]], axis=0)
            wide = mm(both, bh)
            xt[h] += wide[:256] + wide[256:] + mm(both[:256], bl)
        return 0

    lax.fori_loop(0, 8, image, 0)
    for h in range(2):
        hi, lo = split(xt[h].T)
        xhi[h] = hi
        xlo[h] = lo
    def rel_of(k):
        return ((k + 1) // 2 + 2 * (1 - k % 2)) % 4

    def panel_parts(s, pieces):
        bs = [pat[0, 4 * ((y + rel) % 4) + 2 * ab + s] for rel, ab in pieces]
        total = 0.0
        for h in range(2):
            ah = jnp.concatenate([shi[b, h] for b in bs], axis=0)
            al = jnp.concatenate([slo[b, h] for b in bs], axis=0)
            total = total + (mm(ah, xhi[h]) + mm(ah, xlo[h]) + mm(al, xhi[h]))
        return [total[i * 128 : (i + 1) * 128] for i in range(len(pieces))]

    def diag_parts(s, pieces):
        blocks = [ptr[2 * ((y + rel) % 4) + ab, s * 128 : (s + 1) * 128, :] for rel, ab in pieces]
        ah, al = split(jnp.concatenate(blocks, axis=0))
        total = mm(ah, sphi[...]) + mm(ah, splo[...]) + mm(al, sphi[...])
        return [total[i * 128 : (i + 1) * 128] for i in range(len(pieces))]

    def start(q, parts):
        def far(rels):
            for rel, value in zip(rels, parts(1, [(rel, 1 - xh) for rel in rels])):
                vs[q, rel] = value
                send(vs.at[q, rel], vr.at[q, rel], ("v", q, rel), h_dev)

        def near_y(ks):
            for k, value in zip(ks, parts(0, [(rel_of(k), k % 2) for k in ks])):
                psl[q, k] = value

        far((2,))
        near_y((0, 1, 2, 3))
        for d in range(2):
            send(psl.at[q, pl.ds(2 * d, 2)], pr1.at[q, d], ("q", q, d), y_dev[d])
        far((1, 3, 0))
        for rel, value in enumerate(parts(1, [(rel, xh) for rel in range(4)])):
            vo[q, rel, 0] = value[:64]
            vo[q, rel, 1] = value[64:]
        near_y((4, 5, 6, 7))

    def v_add(q, rel):
        arrived(vr.at[q, rel], ("v", q, rel), h_dev)
        vo[q, rel, 0] += vr[q, rel, :64]
        vo[q, rel, 1] += vr[q, rel, 64:]

    def v_first(q):
        v_add(q, 2)
        for d in range(2):
            send(vo.at[q, 2, d], v1.at[q, d], ("v", q, 4 + d), y_dev[d])

    def v_second(q):
        for d, rel in ((0, 1), (1, 3)):
            v_add(q, rel)
            arrived(v1.at[q, d], ("v", q, 4 + d), y_dev[d])
            vo[q, rel, d] += v1[q, d]
            send(vo.at[q, rel], v2.at[q, d], ("v", q, 6 + d), y_dev[d])

    def v_total(q):
        v_add(q, 0)
        for d in range(2):
            arrived(v2.at[q, d], ("v", q, 6 + d), y_dev[d])
        return [vo[q, 0, i] + v2[q, 0, i] + v2[q, 1, i] for i in range(2)]

    def u_combine(q):
        for d, slot in ((0, 6), (1, 5)):
            arrived(pr1.at[q, d], ("q", q, d), y_dev[d])
            psl[q, slot] += pr1[q, d, d]
            send(psl.at[q, slot], pr2.at[q, d], ("q", q, 2 + d), y_dev[d])

    def u_across(q):
        for d in range(2):
            arrived(pr2.at[q, d], ("q", q, 2 + d), y_dev[d])
        psl[q, 4] += pr1[q, 1, 0] + pr2[q, 0]
        psl[q, 7] += pr1[q, 0, 1] + pr2[q, 1]
        send(psl.at[q, 7 - 3 * xh], px.at[q], ("q", q, 4), h_dev)

    def u_total(q):
        arrived(px.at[q], ("q", q, 4), h_dev)
        return psl[q, 4 + 3 * xh] + px[q]

    g_wait(1)
    start(0, panel_parts)
    g_wait(2)
    top_combine(pairs[3])
    v_first(0)
    top_finish(pairs[2])
    top_combine(pairs[4])
    u_combine(0)
    g_wait(3)
    v_second(0)
    u_across(0)
    top_finish(pairs[3])
    top_finish(pairs[4])

    def keep(rows, sp):
        out_panel[rows, :] = sp
        hi, lo = split(sp)
        sphi[rows, :] = hi
        splo[rows, :] = lo

    for i, part in enumerate(v_total(0)):
        keep(slice(128 + 64 * i, 192 + 64 * i), part)
    g_wait(4)
    keep(slice(0, 128), u_total(0))
    keep_panel = pltpu.make_async_copy(out_panel, panel_sum, loads.at[2])
    keep_panel.start()
    start(1, diag_parts)
    v_first(1)
    for p in range(8):
        o = origin(p)
        arrived(xtop.at[o % 4], ("a", p), h_dev, o // 4 == xh)
    for i in range(4):
        out_top[i * 128 : (i + 1) * 128, :] = acc[4 * xh + i] + xtop[i]
    keep_top = pltpu.make_async_copy(out_top, top_sum, loads.at[3])
    keep_top.start()
    u_combine(1)
    v_second(1)
    u_across(1)
    for i, part in enumerate(v_total(1)):
        out_diag[128 + 64 * i : 192 + 64 * i, :] = part
    out_diag[:128, :] = u_total(1)
    keep_diag = pltpu.make_async_copy(out_diag, diag_sum, loads.at[4])
    keep_diag.start()
    for desc in (keep_panel, keep_top, keep_diag):
        desc.wait()
    for desc, cond in sent:
        if cond is None:
            desc.wait_send()
        else:
            pl.when(cond)(desc.wait_send)


def finish(top_in, panel_in, update_in, diag_in, top_out, panel_out, diag_out, top, sp, upd, diag, sems):
    pairs = ((top_in, top), (panel_in, sp), (update_in, upd), (diag_in, diag))
    loads = [pltpu.make_async_copy(a, b, sems.at[i]) for i, (a, b) in enumerate(pairs)]
    for load in loads:
        load.start()
    loads[0].wait()
    stores = [pltpu.make_async_copy(top, top_out, sems.at[4])]
    stores[0].start()
    loads[1].wait()
    sp[...] = -sp[...]
    stores.append(pltpu.make_async_copy(sp, panel_out.at[0], sems.at[5]))
    stores[1].start()
    loads[2].wait()
    loads[3].wait()
    upd[...] = diag[0] + upd[...]
    stores.append(pltpu.make_async_copy(upd, diag_out.at[0], sems.at[6]))
    stores[2].start()
    for store in stores:
        store.wait()


def per_device(top_inverse, pattern, panel, diag_inverse):
    hbm = pl.BlockSpec(memory_space=pl.ANY)
    smem = pl.BlockSpec(memory_space=pltpu.SMEM)
    dma, f32, b16 = pltpu.SemaphoreType.DMA, lambda *n: pltpu.VMEM(n, F32), lambda *n: pltpu.VMEM(n, BF16)
    shape = lambda *n: jax.ShapeDtypeStruct(n, F32)
    counts = ((2, 4, 4), (10,), (8, 3), (8, 4), (2, 5), (2, 8), (2, 4, 2), (8,), (1,))
    sums = pl.pallas_call(
        kernel,
        out_shape=(shape(512, 128), shape(256, 256), shape(256, 256)),
        in_specs=[smem, hbm, hbm],
        out_specs=(hbm, hbm, hbm),
        scratch_shapes=[
            f32(2, 256, 128), f32(256, 128), f32(1, 2048, 256), f32(512, 128), f32(256, 256), f32(256, 256),
            f32(32, 2, 128, 256), b16(32, 2, 128, 256), b16(32, 2, 128, 256),
            b16(2, 256, 256), f32(8, 256, 256), b16(8, 512, 256),
            f32(2, 256, 256), b16(2, 256, 256), b16(2, 256, 256),
            f32(8, 8, 64, 128), f32(8, 2, 2, 64, 128), f32(8, 2, 64, 128),
            f32(8, 128, 128), f32(4, 128, 128),
            f32(2, 8, 128, 256), f32(2, 2, 2, 128, 256), f32(2, 2, 128, 256), f32(2, 128, 256),
            f32(2, 4, 128, 256), f32(2, 4, 2, 64, 256), f32(2, 4, 128, 256),
            f32(2, 2, 64, 256), f32(2, 2, 2, 64, 256),
            b16(256, 256), b16(256, 256),
            dma((6,)), *(dma(n) for n in counts for _ in range(2)),
        ],
        compiler_params=pltpu.CompilerParams(
            collective_id=0, has_side_effects=True, vmem_limit_bytes=60 * 2**20
        ),
    )(pattern, top_inverse, panel)
    return pl.pallas_call(
        finish,
        out_shape=(shape(512, 128), shape(1, 256, 256), shape(1, 256, 256)),
        in_specs=[hbm] * 4,
        out_specs=(hbm, hbm, hbm),
        scratch_shapes=[f32(512, 128), f32(256, 256), f32(256, 256), f32(1, 256, 256), dma((7,))],
    )(*sums, diag_inverse)


def solution(mesh):
    return jax.shard_map(
        per_device,
        mesh=mesh,
        in_specs=(P("row", ("leaf", "col")), P("leaf", None), P("leaf", None, "col"), P("leaf", "row", "col")),
        out_specs=(P("row", ("leaf", "col")), P("leaf", "row", "col"), P("leaf", "row", "col")),
        check_vma=False,
    )
```

```python
import jax
import jax.numpy as jnp
from jax import lax
from jax.experimental import pallas as pl
from jax.experimental.pallas import tpu as pltpu
from jax.sharding import PartitionSpec as P

F32, BF16 = jnp.float32, jnp.bfloat16
NZ, NY = 8, 4


def split(x):
    hi = x.astype(BF16)
    return hi, (x - hi.astype(F32)).astype(BF16)


def mm(a, b):
    return jnp.dot(a, b, preferred_element_type=F32)


def kernel(
    pat, top_hbm, panel_hbm, top_sum, panel_sum, diag_sum,
    kept, given, panel, out_top, out_panel, out_diag, slab, shi, slo, jcat, ptr, pt, xt, xhi, xlo,
    tsl, tr1, tr2, acc, xtop, psl, pr1, pr2, px, vs, vo, vr, v1, v2, sphi, splo,
    loads, *sems,
):
    names = "zxctqvgaw"
    leaf, row, col = lax.axis_index("leaf"), lax.axis_index("row"), lax.axis_index("col")
    y, xh = row // 2, row % 2
    mod8 = lambda k: (col + k + 16) % 8
    z_dev = ({"col": mod8(1)}, {"col": mod8(-1)})
    y_dev = ({"row": (row + 2) % 8}, {"row": (row + 6) % 8})
    xl = (leaf + 2) % 4
    x_dev = {"leaf": xl}
    lc = leaf + 1 - 2 * (leaf % 2)
    lx = (lc + 2) % 4
    c_dev = {"leaf": lc}
    h_dev = {"row": row + 1 - 2 * xh}

    light = 1 - y // 2
    mate = (3 - y) * 2 + xh
    low, high = row * light + mate * (1 - light), row * (1 - light) + mate * light
    l0 = leaf % 2

    def has(b, h):
        return b // 4 <= (low if h else high)

    fetch_kept = pltpu.make_async_copy(top_hbm.at[pl.ds(0, 256)], kept.at[light], loads.at[0])
    fetch_given = pltpu.make_async_copy(top_hbm.at[pl.ds(256, 256)], given, loads.at[5])
    fetch_panel = pltpu.make_async_copy(panel_hbm, panel, loads.at[1])
    fetch_kept.start()
    fetch_given.start()
    fetch_panel.start()
    sem = pltpu.get_barrier_semaphore()
    peers = (*z_dev, *y_dev, x_dev, c_dev, h_dev)
    for dev in peers:
        pl.semaphore_signal(sem, inc=1, device_id=dev, device_id_type=pl.DeviceIdType.MESH)

    zeros = jnp.zeros((128, 256), F32)

    def clear(i, _):
        shi[16 + i, 1] = zeros.astype(BF16)
        slo[16 + i, 1] = zeros.astype(BF16)
        return 0

    def clear_own(o, _):
        for b, h in ((leaf * 8 + o, 0), (xl * 8 + o, 0), (l0 * 8 + o, 1)):

            @pl.when(jnp.logical_not(has(b, h)))
            def _():
                slab[b, h] = zeros

        return 0

    lax.fori_loop(0, 16, clear, 0)
    lax.fori_loop(0, 8, clear_own, 0)

    own = leaf * 8 + col
    fetch_kept.wait()
    slab[own, light] = kept[light].T
    fetch_given.wait()
    pl.semaphore_wait(sem, len(peers))

    sent = []

    def copy(src, dst, key, dev):
        k = names.index(key[0])
        return pltpu.make_async_remote_copy(
            src_ref=src, dst_ref=dst, send_sem=sems[2 * k].at[key[1:]], recv_sem=sems[2 * k + 1].at[key[1:]],
            device_id=dev, device_id_type=pl.DeviceIdType.MESH,
        )

    def send(src, dst, key, dev, cond=None):
        desc = copy(src, dst, key, dev)
        if cond is None:
            desc.start()
        else:
            pl.when(cond)(desc.start)
        sent.append((desc, cond))

    def arrived(dst, key, dev, cond=None):
        desc = copy(dst, dst, key, dev)
        if cond is None:
            desc.wait_recv()
        else:
            pl.when(cond)(desc.wait_recv)

    def origin(p):
        return mod8(0 if p == 0 else -p if p < 4 else p - 3 if p < 7 else 4)

    def z_unit(d, t, u, hop):
        o = mod8((hop - t) if d == 0 else (t - hop))
        b = (leaf, leaf, xl, l0)[u] * 8 + o
        first, rows = ((0, 64), (64, 64), (64, 64), (0, 128))[u]
        if t == 4:
            first, rows = first + rows // 2 * d, rows // 2
        return slab.at[b, u // 3, pl.ds(first, rows)], has(b, u // 3)

    def z_send(d, t, u):
        ref, cond = z_unit(d, t, u, 1)
        send(ref, ref, ("z", d, t - 1, u), z_dev[d], cond)

    def z_wait(d, t, u):
        ref, cond = z_unit(d, t, u, 0)
        arrived(ref, ("z", d, t - 1, u), z_dev[d], cond)

    def x_send(p):
        b = leaf * 8 + origin(p)
        ref = slab.at[b, 0, pl.ds(0, 64)]
        send(ref, ref, ("x", p), x_dev, has(b, 0))

    def x_wait(p):
        b = xl * 8 + origin(p)
        arrived(slab.at[b, 0, pl.ds(0, 64)], ("x", p), x_dev, has(b, 0))

    def c_send(p, k):
        ref = slab.at[(leaf, xl, l0)[k] * 8 + origin(p), k // 2]
        send(ref, ref, ("c", p, k), c_dev)

    def c_wait(p):
        for k in range(3):
            arrived(slab.at[(lc, lx, 1 - l0)[k] * 8 + origin(p), k // 2], ("c", p, k), c_dev)

    def top_slice(p):
        c_wait(p)
        zz = origin(p)
        parts = []
        for h, count in ((0, 4), (1, 2)):
            his, los = [], []
            for far in range(count):
                b = far * 8 + zz
                hi, lo = split(slab[b, h])
                shi[b, h] = hi
                slo[b, h] = lo
                his.append(hi)
                los.append(lo)
            wide = mm(jnp.concatenate(his, axis=0), jcat[h])
            parts.append(wide[:, :128] + wide[:, 128:] + mm(jnp.concatenate(los, axis=0), jcat[h, :, :128]))
        for far in range(4):
            rows = slice(far * 128, (far + 1) * 128)
            t = parts[0][rows] + parts[1][rows] if far < 2 else parts[0][rows]
            rel = (far - y + 4) % 4
            tsl[p, (2 * rel + 4) % 8] = t[:64]
            tsl[p, (2 * rel + 7) % 8] = t[64:]
        for d in range(2):
            send(tsl.at[p, pl.ds(2 * d, 2)], tr1.at[p, d], ("t", p, d), y_dev[d])

    def top_combine(ps):
        for p in ps:
            for d, slot in ((0, 6), (1, 5)):
                arrived(tr1.at[p, d], ("t", p, d), y_dev[d])
                tsl[p, slot] += tr1[p, d, d]
                send(tsl.at[p, slot], tr2.at[p, d], ("t", p, 2 + d), y_dev[d])

    def top_finish(ps):
        for p in ps:
            for d in range(2):
                arrived(tr2.at[p, d], ("t", p, 2 + d), y_dev[d])
            o = origin(p)
            acc[o, :64] = tsl[p, 4] + tr1[p, 1, 0] + tr2[p, 0]
            acc[o, 64:] = tsl[p, 7] + tr1[p, 0, 1] + tr2[p, 1]
            send(acc.at[o], xtop.at[o % 4], ("a", p), h_dev, o // 4 != xh)

    send(given, kept.at[light], ("w", 0), {"row": mate})
    ref_b, ref_l = slab.at[own, 0, pl.ds(64, 64)], slab.at[l0 * 8 + col, 1]
    near = leaf // 2 == 0
    low_here = has(l0 * 8 + col, 1)

    def start_high():
        for d in range(2):
            for u in range(2):
                z_send(d, 1, u)
        send(ref_b, ref_b, ("x", 8), x_dev, has(own, 0))
        x_send(0)
        c_send(0, 0)

    def start_low():
        for d in range(2):
            z_send(d, 1, 3)
        send(ref_l, ref_l, ("x", 9), x_dev, low_here)
        c_send(0, 2)

    mark = len(sent)
    pl.when(light == 0)(start_high)
    pl.when(jnp.logical_and(light == 1, near))(start_low)
    del sent[mark:]
    fetch_panel.wait()

    def turn(i, _):
        block = panel[0, pl.ds(pl.multiple_of(i * 256, 256), 256), :].T
        hi, lo = split(block)
        pt[i, :256] = hi
        pt[i, 256:] = lo
        return 0

    lax.fori_loop(0, 8, turn, 0)
    ptr[col] = panel[0, pl.ds(pl.multiple_of(row * 256, 256), 256), :].T
    arrived(kept.at[1 - light], ("w", 0), {"row": mate})
    slab[own, 1 - light] = kept[1 - light].T
    pl.when(light == 1)(start_high)
    pl.when(jnp.logical_and(light == 0, near))(start_low)
    del sent[mark:]
    for h in range(2):
        j_hi, j_lo = split(kept[h])
        jcat[h, :, :128] = j_hi
        jcat[h, :, 128:] = j_lo
    arrived(slab.at[xl * 8 + col, 0, pl.ds(64, 64)], ("x", 8), x_dev, has(xl * 8 + col, 0))
    for d in range(2):
        z_send(d, 1, 2)

    def pass_low():
        arrived(ref_l, ("x", 9), x_dev, low_here)
        for d in range(2):
            z_send(d, 1, 3)
        c_send(0, 2)

    mark = len(sent)
    pl.when(leaf // 2 == 1)(pass_low)
    del sent[mark:]
    for d in range(2):
        for u in (0, 1, 3):
            ref, cond = z_unit(d, 1, u, 1)
            sent.append((copy(ref, ref, ("z", d, 0, u), z_dev[d]), cond))
    sent.append((copy(ref_b, ref_b, ("x", 8), x_dev), has(own, 0)))
    ref = slab.at[own, 0, pl.ds(0, 64)]
    sent.append((copy(ref, ref, ("x", 0), x_dev), has(own, 0)))
    sent.append((copy(ref_l, ref_l, ("x", 9), x_dev), jnp.logical_and(low_here, near)))
    for k, ref in ((0, slab.at[own, 0]), (2, ref_l)):
        sent.append((copy(ref, ref, ("c", 0, k), c_dev), None))

    x_wait(0)
    c_send(0, 1)

    def g_units(t, hop):
        for w in range(2):
            for d in range(2):
                if t < 4 or w == d:
                    o = mod8((hop - t) if d == 0 else (t - hop))
                    yield ptr.at[o, pl.ds(128 * w, 128)], ("g", d, t - 1, w), z_dev[d]

    def g_send(t):
        for ref, key, dev in g_units(t, 1):
            send(ref, ref, key, dev)

    def g_wait(t):
        onward = list(g_units(t + 1, 1)) if t < 3 else list(g_units(4, 1)) if t == 3 else []
        for ref, key, dev in g_units(t, 0):
            arrived(ref, key, dev)
            for out, out_key, out_dev in onward:
                if out_key[1] == key[1] and out_key[3] == key[3]:
                    send(out, out, out_key, out_dev)

    pairs = {0: (0,), 1: (1, 4), 2: (2, 5), 3: (3, 6), 4: (7,)}
    for t in range(1, 5):
        for u in range(4):
            for d in range(2):
                z_wait(d, t, u)
                if t < 4:
                    z_send(d, t + 1, u)
            for p in pairs[t]:
                if u == 0:
                    x_send(p)
                if u % 2:
                    c_send(p, u - 1)
            for i, p in enumerate(pairs[t - 1]):
                if u == (1, 2)[i]:
                    top_slice(p)
            if u == 3 and t >= 2:
                top_combine(pairs[t - 2])
            if u == 3 and t >= 3:
                top_finish(pairs[t - 3])
        for p in pairs[t]:
            x_wait(p)
            c_send(p, 1)
        if t == 3:
            g_send(1)

    top_slice(7)

    for h in range(2):
        xt[h] = jnp.zeros((256, 256), F32)

    def image(i, _):
        b0, b1 = pat[0, 2 * i], pat[0, 2 * i + 1]
        both = pt[i]
        for h in range(2):
            bh = jnp.concatenate([shi[b0, h], shi[b1, h]], axis=0)
            bl = jnp.concatenate([slo[b0, h], slo[b1, h]], axis=0)
            wide = mm(both, bh)
            xt[h] += wide[:256] + wide[256:] + mm(both[:256], bl)
        return 0

    lax.fori_loop(0, 8, image, 0)
    for h in range(2):
        hi, lo = split(xt[h].T)
        xhi[h] = hi
        xlo[h] = lo
    def rel_of(k):
        return ((k + 1) // 2 + 2 * (1 - k % 2)) % 4

    def panel_parts(s, pieces):
        bs = [pat[0, 4 * ((y + rel) % 4) + 2 * ab + s] for rel, ab in pieces]
        total = 0.0
        for h in range(2):
            ah = jnp.concatenate([shi[b, h] for b in bs], axis=0)
            al = jnp.concatenate([slo[b, h] for b in bs], axis=0)
            total = total + (mm(ah, xhi[h]) + mm(ah, xlo[h]) + mm(al, xhi[h]))
        return [total[i * 128 : (i + 1) * 128] for i in range(len(pieces))]

    def diag_parts(s, pieces):
        blocks = [ptr[2 * ((y + rel) % 4) + ab, s * 128 : (s + 1) * 128, :] for rel, ab in pieces]
        ah, al = split(jnp.concatenate(blocks, axis=0))
        total = mm(ah, sphi[...]) + mm(ah, splo[...]) + mm(al, sphi[...])
        return [total[i * 128 : (i + 1) * 128] for i in range(len(pieces))]

    def start(q, parts):
        def far(rels):
            for rel, value in zip(rels, parts(1, [(rel, 1 - xh) for rel in rels])):
                vs[q, rel] = value
                send(vs.at[q, rel], vr.at[q, rel], ("v", q, rel), h_dev)

        def near_y(ks):
            for k, value in zip(ks, parts(0, [(rel_of(k), k % 2) for k in ks])):
                psl[q, k] = value

        far((2,))
        near_y((0, 1, 2, 3))
        for d in range(2):
            send(psl.at[q, pl.ds(2 * d, 2)], pr1.at[q, d], ("q", q, d), y_dev[d])
        far((1, 3, 0))
        for rel, value in enumerate(parts(1, [(rel, xh) for rel in range(4)])):
            vo[q, rel, 0] = value[:64]
            vo[q, rel, 1] = value[64:]
        near_y((4, 5, 6, 7))

    def v_add(q, rel):
        arrived(vr.at[q, rel], ("v", q, rel), h_dev)
        vo[q, rel, 0] += vr[q, rel, :64]
        vo[q, rel, 1] += vr[q, rel, 64:]

    def v_first(q):
        v_add(q, 2)
        for d in range(2):
            send(vo.at[q, 2, d], v1.at[q, d], ("v", q, 4 + d), y_dev[d])

    def v_second(q):
        for d, rel in ((0, 1), (1, 3)):
            v_add(q, rel)
            arrived(v1.at[q, d], ("v", q, 4 + d), y_dev[d])
            vo[q, rel, d] += v1[q, d]
            send(vo.at[q, rel], v2.at[q, d], ("v", q, 6 + d), y_dev[d])

    def v_total(q):
        v_add(q, 0)
        for d in range(2):
            arrived(v2.at[q, d], ("v", q, 6 + d), y_dev[d])
        return [vo[q, 0, i] + v2[q, 0, i] + v2[q, 1, i] for i in range(2)]

    def u_combine(q):
        for d, slot in ((0, 6), (1, 5)):
            arrived(pr1.at[q, d], ("q", q, d), y_dev[d])
            psl[q, slot] += pr1[q, d, d]
            send(psl.at[q, slot], pr2.at[q, d], ("q", q, 2 + d), y_dev[d])

    def u_across(q):
        for d in range(2):
            arrived(pr2.at[q, d], ("q", q, 2 + d), y_dev[d])
        psl[q, 4] += pr1[q, 1, 0] + pr2[q, 0]
        psl[q, 7] += pr1[q, 0, 1] + pr2[q, 1]
        send(psl.at[q, 7 - 3 * xh], px.at[q], ("q", q, 4), h_dev)

    def u_total(q):
        arrived(px.at[q], ("q", q, 4), h_dev)
        return psl[q, 4 + 3 * xh] + px[q]

    g_wait(1)
    start(0, panel_parts)
    g_wait(2)
    v_first(0)
    u_combine(0)
    top_combine(pairs[3])
    top_finish(pairs[2])
    g_wait(3)
    v_second(0)
    u_across(0)
    top_combine(pairs[4])
    top_finish(pairs[3])
    top_finish(pairs[4])

    def keep(rows, sp):
        out_panel[rows, :] = sp
        hi, lo = split(sp)
        sphi[rows, :] = hi
        splo[rows, :] = lo

    for i, part in enumerate(v_total(0)):
        keep(slice(128 + 64 * i, 192 + 64 * i), part)
    g_wait(4)
    keep(slice(0, 128), u_total(0))
    keep_panel = pltpu.make_async_copy(out_panel, panel_sum, loads.at[2])
    keep_panel.start()
    start(1, diag_parts)
    v_first(1)
    for p in range(8):
        o = origin(p)
        arrived(xtop.at[o % 4], ("a", p), h_dev, o // 4 == xh)
    for i in range(4):
        out_top[i * 128 : (i + 1) * 128, :] = acc[4 * xh + i] + xtop[i]
    keep_top = pltpu.make_async_copy(out_top, top_sum, loads.at[3])
    keep_top.start()
    u_combine(1)
    v_second(1)
    u_across(1)
    for i, part in enumerate(v_total(1)):
        out_diag[128 + 64 * i : 192 + 64 * i, :] = part
    out_diag[:128, :] = u_total(1)
    keep_diag = pltpu.make_async_copy(out_diag, diag_sum, loads.at[4])
    keep_diag.start()
    for desc in (keep_panel, keep_top, keep_diag):
        desc.wait()
    for desc, cond in sent:
        if cond is None:
            desc.wait_send()
        else:
            pl.when(cond)(desc.wait_send)


def finish(top_in, panel_in, update_in, diag_in, top_out, panel_out, diag_out, top, sp, upd, diag, sems):
    pairs = ((top_in, top), (panel_in, sp), (update_in, upd), (diag_in, diag))
    loads = [pltpu.make_async_copy(a, b, sems.at[i]) for i, (a, b) in enumerate(pairs)]
    for load in loads:
        load.start()
    loads[0].wait()
    stores = [pltpu.make_async_copy(top, top_out, sems.at[4])]
    stores[0].start()
    loads[1].wait()
    sp[...] = -sp[...]
    stores.append(pltpu.make_async_copy(sp, panel_out.at[0], sems.at[5]))
    stores[1].start()
    loads[2].wait()
    loads[3].wait()
    upd[...] = diag[0] + upd[...]
    stores.append(pltpu.make_async_copy(upd, diag_out.at[0], sems.at[6]))
    stores[2].start()
    for store in stores:
        store.wait()


def per_device(top_inverse, pattern, panel, diag_inverse):
    hbm = pl.BlockSpec(memory_space=pl.ANY)
    smem = pl.BlockSpec(memory_space=pltpu.SMEM)
    dma, f32, b16 = pltpu.SemaphoreType.DMA, lambda *n: pltpu.VMEM(n, F32), lambda *n: pltpu.VMEM(n, BF16)
    shape = lambda *n: jax.ShapeDtypeStruct(n, F32)
    counts = ((2, 4, 4), (10,), (8, 3), (8, 4), (2, 5), (2, 8), (2, 4, 2), (8,), (1,))
    sums = pl.pallas_call(
        kernel,
        out_shape=(shape(512, 128), shape(256, 256), shape(256, 256)),
        in_specs=[smem, hbm, hbm],
        out_specs=(hbm, hbm, hbm),
        scratch_shapes=[
            f32(2, 256, 128), f32(256, 128), f32(1, 2048, 256), f32(512, 128), f32(256, 256), f32(256, 256),
            f32(32, 2, 128, 256), b16(32, 2, 128, 256), b16(32, 2, 128, 256),
            b16(2, 256, 256), f32(8, 256, 256), b16(8, 512, 256),
            f32(2, 256, 256), b16(2, 256, 256), b16(2, 256, 256),
            f32(8, 8, 64, 128), f32(8, 2, 2, 64, 128), f32(8, 2, 64, 128),
            f32(8, 128, 128), f32(4, 128, 128),
            f32(2, 8, 128, 256), f32(2, 2, 2, 128, 256), f32(2, 2, 128, 256), f32(2, 128, 256),
            f32(2, 4, 128, 256), f32(2, 4, 2, 64, 256), f32(2, 4, 128, 256),
            f32(2, 2, 64, 256), f32(2, 2, 2, 64, 256),
            b16(256, 256), b16(256, 256),
            dma((6,)), *(dma(n) for n in counts for _ in range(2)),
        ],
        compiler_params=pltpu.CompilerParams(
            collective_id=0, has_side_effects=True, vmem_limit_bytes=60 * 2**20
        ),
    )(pattern, top_inverse, panel)
    return pl.pallas_call(
        finish,
        out_shape=(shape(512, 128), shape(1, 256, 256), shape(1, 256, 256)),
        in_specs=[hbm] * 4,
        out_specs=(hbm, hbm, hbm),
        scratch_shapes=[f32(512, 128), f32(256, 256), f32(256, 256), f32(1, 256, 256), dma((7,))],
    )(*sums, diag_inverse)


def solution(mesh):
    return jax.shard_map(
        per_device,
        mesh=mesh,
        in_specs=(P("row", ("leaf", "col")), P("leaf", None), P("leaf", None, "col"), P("leaf", "row", "col")),
        out_specs=(P("row", ("leaf", "col")), P("leaf", "row", "col"), P("leaf", "row", "col")),
        check_vma=False,
    )
```

```python
import jax
import jax.numpy as jnp
from jax import lax
from jax.experimental import pallas as pl
from jax.experimental.pallas import tpu as pltpu
from jax.sharding import PartitionSpec as P

F32, BF16 = jnp.float32, jnp.bfloat16
NZ, NY = 8, 4


def split(x):
    hi = x.astype(BF16)
    return hi, (x - hi.astype(F32)).astype(BF16)


def mm(a, b):
    return jnp.dot(a, b, preferred_element_type=F32)


def kernel(
    pat, top_hbm, panel_hbm, top_sum, panel_sum, diag_sum,
    kept, given, panel, out_top, out_panel, out_diag, slab, shi, slo, jcat, ptr, pt, xt, xhi, xlo,
    tsl, tr1, tr2, acc, xtop, psl, pr1, pr2, px, vs, vo, vr, v1, v2, sphi, splo,
    loads, *sems,
):
    names = "zxctqvgaw"
    leaf, row, col = lax.axis_index("leaf"), lax.axis_index("row"), lax.axis_index("col")
    y, xh = row // 2, row % 2
    mod8 = lambda k: (col + k + 16) % 8
    z_dev = ({"col": mod8(1)}, {"col": mod8(-1)})
    y_dev = ({"row": (row + 2) % 8}, {"row": (row + 6) % 8})
    xl = (leaf + 2) % 4
    x_dev = {"leaf": xl}
    lc = leaf + 1 - 2 * (leaf % 2)
    lx = (lc + 2) % 4
    c_dev = {"leaf": lc}
    h_dev = {"row": row + 1 - 2 * xh}

    light = 1 - y // 2
    mate = (3 - y) * 2 + xh
    low, high = row * light + mate * (1 - light), row * (1 - light) + mate * light
    l0 = leaf % 2

    def has(b, h):
        return b // 4 <= (low if h else high)

    fetch_kept = pltpu.make_async_copy(top_hbm.at[pl.ds(0, 256)], kept.at[light], loads.at[0])
    fetch_given = pltpu.make_async_copy(top_hbm.at[pl.ds(256, 256)], given, loads.at[5])
    fetch_panel = pltpu.make_async_copy(panel_hbm, panel, loads.at[1])
    fetch_kept.start()
    fetch_given.start()
    fetch_panel.start()
    sem = pltpu.get_barrier_semaphore()
    peers = (*z_dev, *y_dev, x_dev, c_dev, h_dev)
    for dev in peers:
        pl.semaphore_signal(sem, inc=1, device_id=dev, device_id_type=pl.DeviceIdType.MESH)

    zeros = jnp.zeros((128, 256), F32)

    def clear(i, _):
        shi[16 + i, 1] = zeros.astype(BF16)
        slo[16 + i, 1] = zeros.astype(BF16)
        return 0

    def clear_own(o, _):
        for b, h in ((leaf * 8 + o, 0), (xl * 8 + o, 0), (l0 * 8 + o, 1)):

            @pl.when(jnp.logical_not(has(b, h)))
            def _():
                slab[b, h] = zeros

        return 0

    lax.fori_loop(0, 16, clear, 0)
    lax.fori_loop(0, 8, clear_own, 0)

    own = leaf * 8 + col
    fetch_kept.wait()
    slab[own, light] = kept[light].T
    fetch_given.wait()
    pl.semaphore_wait(sem, len(peers))

    sent = []

    def copy(src, dst, key, dev):
        k = names.index(key[0])
        return pltpu.make_async_remote_copy(
            src_ref=src, dst_ref=dst, send_sem=sems[2 * k].at[key[1:]], recv_sem=sems[2 * k + 1].at[key[1:]],
            device_id=dev, device_id_type=pl.DeviceIdType.MESH,
        )

    def send(src, dst, key, dev, cond=None):
        desc = copy(src, dst, key, dev)
        if cond is None:
            desc.start()
        else:
            pl.when(cond)(desc.start)
        sent.append((desc, cond))

    def arrived(dst, key, dev, cond=None):
        desc = copy(dst, dst, key, dev)
        if cond is None:
            desc.wait_recv()
        else:
            pl.when(cond)(desc.wait_recv)

    def origin(p):
        return mod8(0 if p == 0 else -p if p < 4 else p - 3 if p < 7 else 4)

    def z_unit(d, t, u, hop):
        o = mod8((hop - t) if d == 0 else (t - hop))
        b = (leaf, leaf, xl, l0)[u] * 8 + o
        first, rows = ((0, 64), (64, 64), (64, 64), (0, 128))[u]
        if t == 4:
            first, rows = first + rows // 2 * d, rows // 2
        return slab.at[b, u // 3, pl.ds(first, rows)], has(b, u // 3)

    def z_send(d, t, u):
        ref, cond = z_unit(d, t, u, 1)
        send(ref, ref, ("z", d, t - 1, u), z_dev[d], cond)

    def z_wait(d, t, u):
        ref, cond = z_unit(d, t, u, 0)
        arrived(ref, ("z", d, t - 1, u), z_dev[d], cond)

    def x_send(p):
        b = leaf * 8 + origin(p)
        ref = slab.at[b, 0, pl.ds(0, 64)]
        send(ref, ref, ("x", p), x_dev, has(b, 0))

    def x_wait(p):
        b = xl * 8 + origin(p)
        arrived(slab.at[b, 0, pl.ds(0, 64)], ("x", p), x_dev, has(b, 0))

    def c_send(p, k):
        ref = slab.at[(leaf, xl, l0)[k] * 8 + origin(p), k // 2]
        send(ref, ref, ("c", p, k), c_dev)

    def c_wait(p):
        for k in range(3):
            arrived(slab.at[(lc, lx, 1 - l0)[k] * 8 + origin(p), k // 2], ("c", p, k), c_dev)

    def top_slice(p):
        c_wait(p)
        zz = origin(p)
        parts = []
        for h, count in ((0, 4), (1, 2)):
            his, los = [], []
            for far in range(count):
                b = far * 8 + zz
                hi, lo = split(slab[b, h])
                shi[b, h] = hi
                slo[b, h] = lo
                his.append(hi)
                los.append(lo)
            wide = mm(jnp.concatenate(his, axis=0), jcat[h])
            parts.append(wide[:, :128] + wide[:, 128:] + mm(jnp.concatenate(los, axis=0), jcat[h, :, :128]))
        for far in range(4):
            rows = slice(far * 128, (far + 1) * 128)
            t = parts[0][rows] + parts[1][rows] if far < 2 else parts[0][rows]
            rel = (far - y + 4) % 4
            tsl[p, (2 * rel + 4) % 8] = t[:64]
            tsl[p, (2 * rel + 7) % 8] = t[64:]
        for d in range(2):
            send(tsl.at[p, pl.ds(2 * d, 2)], tr1.at[p, d], ("t", p, d), y_dev[d])

    def top_combine(ps):
        for p in ps:
            for d, slot in ((0, 6), (1, 5)):
                arrived(tr1.at[p, d], ("t", p, d), y_dev[d])
                tsl[p, slot] += tr1[p, d, d]
                send(tsl.at[p, slot], tr2.at[p, d], ("t", p, 2 + d), y_dev[d])

    def top_finish(ps):
        for p in ps:
            for d in range(2):
                arrived(tr2.at[p, d], ("t", p, 2 + d), y_dev[d])
            o = origin(p)
            acc[o, :64] = tsl[p, 4] + tr1[p, 1, 0] + tr2[p, 0]
            acc[o, 64:] = tsl[p, 7] + tr1[p, 0, 1] + tr2[p, 1]
            send(acc.at[o], xtop.at[o % 4], ("a", p), h_dev, o // 4 != xh)

    send(given, kept.at[light], ("w", 0), {"row": mate})
    ref_b, ref_l = slab.at[own, 0, pl.ds(64, 64)], slab.at[l0 * 8 + col, 1]
    near = leaf // 2 == 0
    low_here = has(l0 * 8 + col, 1)

    def start_high():
        for d in range(2):
            for u in range(2):
                z_send(d, 1, u)
        send(ref_b, ref_b, ("x", 8), x_dev, has(own, 0))
        x_send(0)
        c_send(0, 0)

    def start_low():
        for d in range(2):
            z_send(d, 1, 3)
        send(ref_l, ref_l, ("x", 9), x_dev, low_here)
        c_send(0, 2)

    mark = len(sent)
    pl.when(light == 0)(start_high)
    pl.when(jnp.logical_and(light == 1, near))(start_low)
    del sent[mark:]
    fetch_panel.wait()

    def turn(i, _):
        block = panel[0, pl.ds(pl.multiple_of(i * 256, 256), 256), :].T
        hi, lo = split(block)
        pt[i, :256] = hi
        pt[i, 256:] = lo
        return 0

    lax.fori_loop(0, 8, turn, 0)
    ptr[col] = panel[0, pl.ds(pl.multiple_of(row * 256, 256), 256), :].T
    arrived(kept.at[1 - light], ("w", 0), {"row": mate})
    slab[own, 1 - light] = kept[1 - light].T
    pl.when(light == 1)(start_high)
    pl.when(jnp.logical_and(light == 0, near))(start_low)
    del sent[mark:]
    for h in range(2):
        j_hi, j_lo = split(kept[h])
        jcat[h, :, :128] = j_hi
        jcat[h, :, 128:] = j_lo
    arrived(slab.at[xl * 8 + col, 0, pl.ds(64, 64)], ("x", 8), x_dev, has(xl * 8 + col, 0))
    for d in range(2):
        z_send(d, 1, 2)

    def pass_low():
        arrived(ref_l, ("x", 9), x_dev, low_here)
        for d in range(2):
            z_send(d, 1, 3)
        c_send(0, 2)

    mark = len(sent)
    pl.when(leaf // 2 == 1)(pass_low)
    del sent[mark:]
    for d in range(2):
        for u in (0, 1, 3):
            ref, cond = z_unit(d, 1, u, 1)
            sent.append((copy(ref, ref, ("z", d, 0, u), z_dev[d]), cond))
    sent.append((copy(ref_b, ref_b, ("x", 8), x_dev), has(own, 0)))
    ref = slab.at[own, 0, pl.ds(0, 64)]
    sent.append((copy(ref, ref, ("x", 0), x_dev), has(own, 0)))
    sent.append((copy(ref_l, ref_l, ("x", 9), x_dev), jnp.logical_and(low_here, near)))
    for k, ref in ((0, slab.at[own, 0]), (2, ref_l)):
        sent.append((copy(ref, ref, ("c", 0, k), c_dev), None))

    x_wait(0)
    c_send(0, 1)

    def g_units(t, hop):
        for w in range(2):
            for d in range(2):
                if t < 4 or w == d:
                    o = mod8((hop - t) if d == 0 else (t - hop))
                    yield ptr.at[o, pl.ds(128 * w, 128)], ("g", d, t - 1, w), z_dev[d]

    def g_send(t):
        for ref, key, dev in g_units(t, 1):
            send(ref, ref, key, dev)

    def g_wait(t):
        onward = list(g_units(t + 1, 1)) if t < 3 else list(g_units(4, 1)) if t == 3 else []
        for ref, key, dev in g_units(t, 0):
            arrived(ref, key, dev)
            for out, out_key, out_dev in onward:
                if out_key[1] == key[1] and out_key[3] == key[3]:
                    send(out, out, out_key, out_dev)

    pairs = {0: (0,), 1: (1, 4), 2: (2, 5), 3: (3, 6), 4: (7,)}
    for t in range(1, 5):
        for u in range(4):
            for d in range(2):
                z_wait(d, t, u)
                if t < 4:
                    z_send(d, t + 1, u)
            for p in pairs[t]:
                if u == 0:
                    x_send(p)
                if u % 2:
                    c_send(p, u - 1)
            for i, p in enumerate(pairs[t - 1]):
                if u == (1, 2)[i]:
                    top_slice(p)
            if u == 3 and t >= 2:
                top_combine(pairs[t - 2])
            if u == 3 and t >= 3:
                top_finish(pairs[t - 3])
        for p in pairs[t]:
            x_wait(p)
            c_send(p, 1)
        if t == 3:
            g_send(1)

    top_slice(7)

    for h in range(2):
        xt[h] = jnp.zeros((256, 256), F32)

    def image(i, _):
        b0, b1 = pat[0, 2 * i], pat[0, 2 * i + 1]
        both = pt[i]
        for h in range(2):
            bh = jnp.concatenate([shi[b0, h], shi[b1, h]], axis=0)
            bl = jnp.concatenate([slo[b0, h], slo[b1, h]], axis=0)
            wide = mm(both, bh)
            xt[h] += wide[:256] + wide[256:] + mm(both[:256], bl)
        return 0

    lax.fori_loop(0, 8, image, 0)
    for h in range(2):
        hi, lo = split(xt[h].T)
        xhi[h] = hi
        xlo[h] = lo
    def rel_of(k):
        return ((k + 1) // 2 + 2 * (1 - k % 2)) % 4

    def panel_parts(s, pieces):
        bs = [pat[0, 4 * ((y + rel) % 4) + 2 * ab + s] for rel, ab in pieces]
        total = 0.0
        for h in range(2):
            ah = jnp.concatenate([shi[b, h] for b in bs], axis=0)
            al = jnp.concatenate([slo[b, h] for b in bs], axis=0)
            total = total + (mm(ah, xhi[h]) + mm(ah, xlo[h]) + mm(al, xhi[h]))
        return [total[i * 128 : (i + 1) * 128] for i in range(len(pieces))]

    def diag_parts(s, pieces):
        blocks = [ptr[2 * ((y + rel) % 4) + ab, s * 128 : (s + 1) * 128, :] for rel, ab in pieces]
        ah, al = split(jnp.concatenate(blocks, axis=0))
        total = mm(ah, sphi[...]) + mm(ah, splo[...]) + mm(al, sphi[...])
        return [total[i * 128 : (i + 1) * 128] for i in range(len(pieces))]

    def start(q, parts):
        def far(rels):
            for rel, value in zip(rels, parts(1, [(rel, 1 - xh) for rel in rels])):
                vs[q, rel] = value
                send(vs.at[q, rel], vr.at[q, rel], ("v", q, rel), h_dev)

        def near_y(ks):
            for k, value in zip(ks, parts(0, [(rel_of(k), k % 2) for k in ks])):
                psl[q, k] = value

        near_y((0, 1, 2, 3))
        for d in range(2):
            send(psl.at[q, pl.ds(2 * d, 2)], pr1.at[q, d], ("q", q, d), y_dev[d])
        far((2, 1, 3, 0))
        for rel, value in enumerate(parts(1, [(rel, xh) for rel in range(4)])):
            vo[q, rel, 0] = value[:64]
            vo[q, rel, 1] = value[64:]
        near_y((4, 5, 6, 7))

    def v_add(q, rel):
        arrived(vr.at[q, rel], ("v", q, rel), h_dev)
        vo[q, rel, 0] += vr[q, rel, :64]
        vo[q, rel, 1] += vr[q, rel, 64:]

    def v_first(q):
        v_add(q, 2)
        for d in range(2):
            send(vo.at[q, 2, d], v1.at[q, d], ("v", q, 4 + d), y_dev[d])

    def v_second(q):
        for d, rel in ((0, 1), (1, 3)):
            v_add(q, rel)
            arrived(v1.at[q, d], ("v", q, 4 + d), y_dev[d])
            vo[q, rel, d] += v1[q, d]
            send(vo.at[q, rel], v2.at[q, d], ("v", q, 6 + d), y_dev[d])

    def v_total(q):
        v_add(q, 0)
        for d in range(2):
            arrived(v2.at[q, d], ("v", q, 6 + d), y_dev[d])
        return [vo[q, 0, i] + v2[q, 0, i] + v2[q, 1, i] for i in range(2)]

    def u_combine(q):
        for d, slot in ((0, 6), (1, 5)):
            arrived(pr1.at[q, d], ("q", q, d), y_dev[d])
            psl[q, slot] += pr1[q, d, d]
            send(psl.at[q, slot], pr2.at[q, d], ("q", q, 2 + d), y_dev[d])

    def u_across(q):
        for d in range(2):
            arrived(pr2.at[q, d], ("q", q, 2 + d), y_dev[d])
        psl[q, 4] += pr1[q, 1, 0] + pr2[q, 0]
        psl[q, 7] += pr1[q, 0, 1] + pr2[q, 1]
        send(psl.at[q, 7 - 3 * xh], px.at[q], ("q", q, 4), h_dev)

    def u_total(q):
        arrived(px.at[q], ("q", q, 4), h_dev)
        return psl[q, 4 + 3 * xh] + px[q]

    g_wait(1)
    start(0, panel_parts)
    g_wait(2)
    v_first(0)
    u_combine(0)
    top_combine(pairs[3])
    top_finish(pairs[2])
    g_wait(3)
    v_second(0)
    u_across(0)
    top_combine(pairs[4])
    top_finish(pairs[3])
    top_finish(pairs[4])

    def keep(rows, sp):
        out_panel[rows, :] = sp
        hi, lo = split(sp)
        sphi[rows, :] = hi
        splo[rows, :] = lo

    for i, part in enumerate(v_total(0)):
        keep(slice(128 + 64 * i, 192 + 64 * i), part)
    g_wait(4)
    keep(slice(0, 128), u_total(0))
    keep_panel = pltpu.make_async_copy(out_panel, panel_sum, loads.at[2])
    keep_panel.start()
    start(1, diag_parts)
    v_first(1)
    u_combine(1)
    v_second(1)
    u_across(1)
    for p in range(8):
        o = origin(p)
        arrived(xtop.at[o % 4], ("a", p), h_dev, o // 4 == xh)
    for i in range(4):
        out_top[i * 128 : (i + 1) * 128, :] = acc[4 * xh + i] + xtop[i]
    keep_top = pltpu.make_async_copy(out_top, top_sum, loads.at[3])
    keep_top.start()
    for i, part in enumerate(v_total(1)):
        out_diag[128 + 64 * i : 192 + 64 * i, :] = part
    out_diag[:128, :] = u_total(1)
    keep_diag = pltpu.make_async_copy(out_diag, diag_sum, loads.at[4])
    keep_diag.start()
    for desc in (keep_panel, keep_top, keep_diag):
        desc.wait()
    for desc, cond in sent:
        if cond is None:
            desc.wait_send()
        else:
            pl.when(cond)(desc.wait_send)


def finish(top_in, panel_in, update_in, diag_in, top_out, panel_out, diag_out, top, sp, upd, diag, sems):
    pairs = ((top_in, top), (panel_in, sp), (update_in, upd), (diag_in, diag))
    loads = [pltpu.make_async_copy(a, b, sems.at[i]) for i, (a, b) in enumerate(pairs)]
    for load in loads:
        load.start()
    loads[0].wait()
    stores = [pltpu.make_async_copy(top, top_out, sems.at[4])]
    stores[0].start()
    loads[1].wait()
    sp[...] = -sp[...]
    stores.append(pltpu.make_async_copy(sp, panel_out.at[0], sems.at[5]))
    stores[1].start()
    loads[2].wait()
    loads[3].wait()
    upd[...] = diag[0] + upd[...]
    stores.append(pltpu.make_async_copy(upd, diag_out.at[0], sems.at[6]))
    stores[2].start()
    for store in stores:
        store.wait()


def per_device(top_inverse, pattern, panel, diag_inverse):
    hbm = pl.BlockSpec(memory_space=pl.ANY)
    smem = pl.BlockSpec(memory_space=pltpu.SMEM)
    dma, f32, b16 = pltpu.SemaphoreType.DMA, lambda *n: pltpu.VMEM(n, F32), lambda *n: pltpu.VMEM(n, BF16)
    shape = lambda *n: jax.ShapeDtypeStruct(n, F32)
    counts = ((2, 4, 4), (10,), (8, 3), (8, 4), (2, 5), (2, 8), (2, 4, 2), (8,), (1,))
    sums = pl.pallas_call(
        kernel,
        out_shape=(shape(512, 128), shape(256, 256), shape(256, 256)),
        in_specs=[smem, hbm, hbm],
        out_specs=(hbm, hbm, hbm),
        scratch_shapes=[
            f32(2, 256, 128), f32(256, 128), f32(1, 2048, 256), f32(512, 128), f32(256, 256), f32(256, 256),
            f32(32, 2, 128, 256), b16(32, 2, 128, 256), b16(32, 2, 128, 256),
            b16(2, 256, 256), f32(8, 256, 256), b16(8, 512, 256),
            f32(2, 256, 256), b16(2, 256, 256), b16(2, 256, 256),
            f32(8, 8, 64, 128), f32(8, 2, 2, 64, 128), f32(8, 2, 64, 128),
            f32(8, 128, 128), f32(4, 128, 128),
            f32(2, 8, 128, 256), f32(2, 2, 2, 128, 256), f32(2, 2, 128, 256), f32(2, 128, 256),
            f32(2, 4, 128, 256), f32(2, 4, 2, 64, 256), f32(2, 4, 128, 256),
            f32(2, 2, 64, 256), f32(2, 2, 2, 64, 256),
            b16(256, 256), b16(256, 256),
            dma((6,)), *(dma(n) for n in counts for _ in range(2)),
        ],
        compiler_params=pltpu.CompilerParams(
            collective_id=0, has_side_effects=True, vmem_limit_bytes=60 * 2**20
        ),
    )(pattern, top_inverse, panel)
    return pl.pallas_call(
        finish,
        out_shape=(shape(512, 128), shape(1, 256, 256), shape(1, 256, 256)),
        in_specs=[hbm] * 4,
        out_specs=(hbm, hbm, hbm),
        scratch_shapes=[f32(512, 128), f32(256, 256), f32(256, 256), f32(1, 256, 256), dma((7,))],
    )(*sums, diag_inverse)


def solution(mesh):
    return jax.shard_map(
        per_device,
        mesh=mesh,
        in_specs=(P("row", ("leaf", "col")), P("leaf", None), P("leaf", None, "col"), P("leaf", "row", "col")),
        out_specs=(P("row", ("leaf", "col")), P("leaf", "row", "col"), P("leaf", "row", "col")),
        check_vma=False,
    )
```

```python
import jax
import jax.numpy as jnp
from jax import lax
from jax.experimental import pallas as pl
from jax.experimental.pallas import tpu as pltpu
from jax.sharding import PartitionSpec as P

F32, BF16 = jnp.float32, jnp.bfloat16
NZ, NY = 8, 4


def split(x):
    hi = x.astype(BF16)
    return hi, (x - hi.astype(F32)).astype(BF16)


def mm(a, b):
    return jnp.dot(a, b, preferred_element_type=F32)


def kernel(
    pat, top_hbm, panel_hbm, top_sum, panel_sum, diag_sum,
    kept, given, panel, out_top, out_panel, out_diag, slab, shi, slo, jcat, ptr, pt, xt, xhi, xlo,
    tsl, tr1, tr2, acc, xtop, psl, pr1, pr2, px, vs, vo, vr, v1, v2, sphi, splo,
    loads, *sems,
):
    names = "zxctqvgaw"
    leaf, row, col = lax.axis_index("leaf"), lax.axis_index("row"), lax.axis_index("col")
    y, xh = row // 2, row % 2
    mod8 = lambda k: (col + k + 16) % 8
    z_dev = ({"col": mod8(1)}, {"col": mod8(-1)})
    y_dev = ({"row": (row + 2) % 8}, {"row": (row + 6) % 8})
    xl = (leaf + 2) % 4
    x_dev = {"leaf": xl}
    lc = leaf + 1 - 2 * (leaf % 2)
    lx = (lc + 2) % 4
    c_dev = {"leaf": lc}
    h_dev = {"row": row + 1 - 2 * xh}

    light = 1 - y // 2
    mate = (3 - y) * 2 + xh
    low, high = row * light + mate * (1 - light), row * (1 - light) + mate * light
    l0 = leaf % 2

    def has(b, h):
        return b // 4 <= (low if h else high)

    fetch_kept = pltpu.make_async_copy(top_hbm.at[pl.ds(0, 256)], kept.at[light], loads.at[0])
    fetch_given = pltpu.make_async_copy(top_hbm.at[pl.ds(256, 256)], given, loads.at[5])
    fetch_panel = pltpu.make_async_copy(panel_hbm, panel, loads.at[1])
    fetch_kept.start()
    fetch_given.start()
    fetch_panel.start()
    sem = pltpu.get_barrier_semaphore()
    peers = (*z_dev, *y_dev, x_dev, c_dev, h_dev)
    for dev in peers:
        pl.semaphore_signal(sem, inc=1, device_id=dev, device_id_type=pl.DeviceIdType.MESH)

    zeros = jnp.zeros((128, 256), F32)

    def clear(i, _):
        shi[16 + i, 1] = zeros.astype(BF16)
        slo[16 + i, 1] = zeros.astype(BF16)
        return 0

    def clear_own(o, _):
        for b, h in ((leaf * 8 + o, 0), (xl * 8 + o, 0), (l0 * 8 + o, 1)):

            @pl.when(jnp.logical_not(has(b, h)))
            def _():
                slab[b, h] = zeros

        return 0

    lax.fori_loop(0, 16, clear, 0)
    lax.fori_loop(0, 8, clear_own, 0)

    own = leaf * 8 + col
    fetch_kept.wait()
    slab[own, light] = kept[light].T
    fetch_given.wait()
    pl.semaphore_wait(sem, len(peers))

    sent = []

    def copy(src, dst, key, dev):
        k = names.index(key[0])
        return pltpu.make_async_remote_copy(
            src_ref=src, dst_ref=dst, send_sem=sems[2 * k].at[key[1:]], recv_sem=sems[2 * k + 1].at[key[1:]],
            device_id=dev, device_id_type=pl.DeviceIdType.MESH,
        )

    def send(src, dst, key, dev, cond=None):
        desc = copy(src, dst, key, dev)
        if cond is None:
            desc.start()
        else:
            pl.when(cond)(desc.start)
        sent.append((desc, cond))

    def arrived(dst, key, dev, cond=None):
        desc = copy(dst, dst, key, dev)
        if cond is None:
            desc.wait_recv()
        else:
            pl.when(cond)(desc.wait_recv)

    def origin(p):
        return mod8(0 if p == 0 else -p if p < 4 else p - 3 if p < 7 else 4)

    def z_unit(d, t, u, hop):
        o = mod8((hop - t) if d == 0 else (t - hop))
        b = (leaf, leaf, xl, l0)[u] * 8 + o
        first, rows = ((0, 64), (64, 64), (64, 64), (0, 128))[u]
        if t == 4:
            first, rows = first + rows // 2 * d, rows // 2
        return slab.at[b, u // 3, pl.ds(first, rows)], has(b, u // 3)

    def z_send(d, t, u):
        ref, cond = z_unit(d, t, u, 1)
        send(ref, ref, ("z", d, t - 1, u), z_dev[d], cond)

    def z_wait(d, t, u):
        ref, cond = z_unit(d, t, u, 0)
        arrived(ref, ("z", d, t - 1, u), z_dev[d], cond)

    def x_send(p):
        b = leaf * 8 + origin(p)
        ref = slab.at[b, 0, pl.ds(0, 64)]
        send(ref, ref, ("x", p), x_dev, has(b, 0))

    def x_wait(p):
        b = xl * 8 + origin(p)
        arrived(slab.at[b, 0, pl.ds(0, 64)], ("x", p), x_dev, has(b, 0))

    def c_send(p, k):
        ref = slab.at[(leaf, xl, l0)[k] * 8 + origin(p), k // 2]
        send(ref, ref, ("c", p, k), c_dev)

    def c_wait(p):
        for k in range(3):
            arrived(slab.at[(lc, lx, 1 - l0)[k] * 8 + origin(p), k // 2], ("c", p, k), c_dev)

    def top_slice(p):
        c_wait(p)
        zz = origin(p)
        parts = []
        for h, count in ((0, 4), (1, 2)):
            his, los = [], []
            for far in range(count):
                b = far * 8 + zz
                hi, lo = split(slab[b, h])
                shi[b, h] = hi
                slo[b, h] = lo
                his.append(hi)
                los.append(lo)
            wide = mm(jnp.concatenate(his, axis=0), jcat[h])
            parts.append(wide[:, :128] + wide[:, 128:] + mm(jnp.concatenate(los, axis=0), jcat[h, :, :128]))
        for far in range(4):
            rows = slice(far * 128, (far + 1) * 128)
            t = parts[0][rows] + parts[1][rows] if far < 2 else parts[0][rows]
            rel = (far - y + 4) % 4
            tsl[p, (2 * rel + 4) % 8] = t[:64]
            tsl[p, (2 * rel + 7) % 8] = t[64:]
        for d in range(2):
            send(tsl.at[p, pl.ds(2 * d, 2)], tr1.at[p, d], ("t", p, d), y_dev[d])

    def top_combine(ps):
        for p in ps:
            for d, slot in ((0, 6), (1, 5)):
                arrived(tr1.at[p, d], ("t", p, d), y_dev[d])
                tsl[p, slot] += tr1[p, d, d]
                send(tsl.at[p, slot], tr2.at[p, d], ("t", p, 2 + d), y_dev[d])

    def top_finish(ps):
        for p in ps:
            for d in range(2):
                arrived(tr2.at[p, d], ("t", p, 2 + d), y_dev[d])
            o = origin(p)
            acc[o, :64] = tsl[p, 4] + tr1[p, 1, 0] + tr2[p, 0]
            acc[o, 64:] = tsl[p, 7] + tr1[p, 0, 1] + tr2[p, 1]
            send(acc.at[o], xtop.at[o % 4], ("a", p), h_dev, o // 4 != xh)

    send(given, kept.at[light], ("w", 0), {"row": mate})
    ref_b, ref_l = slab.at[own, 0, pl.ds(64, 64)], slab.at[l0 * 8 + col, 1]
    near = leaf // 2 == 0
    low_here = has(l0 * 8 + col, 1)

    def start_high():
        for d in range(2):
            for u in range(2):
                z_send(d, 1, u)
        send(ref_b, ref_b, ("x", 8), x_dev, has(own, 0))
        x_send(0)
        c_send(0, 0)

    def start_low():
        for d in range(2):
            z_send(d, 1, 3)
        send(ref_l, ref_l, ("x", 9), x_dev, low_here)
        c_send(0, 2)

    mark = len(sent)
    pl.when(light == 0)(start_high)
    pl.when(jnp.logical_and(light == 1, near))(start_low)
    del sent[mark:]
    def split_own(h):
        j_hi, j_lo = split(kept[h])
        jcat[h, :, :128] = j_hi
        jcat[h, :, 128:] = j_lo

    split_own(light)
    fetch_panel.wait()

    def turn(i, _):
        block = panel[0, pl.ds(pl.multiple_of(i * 256, 256), 256), :].T
        hi, lo = split(block)
        pt[i, :256] = hi
        pt[i, 256:] = lo
        return 0

    lax.fori_loop(0, 8, turn, 0)
    ptr[col] = panel[0, pl.ds(pl.multiple_of(row * 256, 256), 256), :].T
    arrived(kept.at[1 - light], ("w", 0), {"row": mate})
    slab[own, 1 - light] = kept[1 - light].T
    pl.when(light == 1)(start_high)
    pl.when(jnp.logical_and(light == 0, near))(start_low)
    del sent[mark:]
    split_own(1 - light)
    arrived(slab.at[xl * 8 + col, 0, pl.ds(64, 64)], ("x", 8), x_dev, has(xl * 8 + col, 0))
    for d in range(2):
        z_send(d, 1, 2)

    def pass_low():
        arrived(ref_l, ("x", 9), x_dev, low_here)
        for d in range(2):
            z_send(d, 1, 3)
        c_send(0, 2)

    mark = len(sent)
    pl.when(leaf // 2 == 1)(pass_low)
    del sent[mark:]
    for d in range(2):
        for u in (0, 1, 3):
            ref, cond = z_unit(d, 1, u, 1)
            sent.append((copy(ref, ref, ("z", d, 0, u), z_dev[d]), cond))
    sent.append((copy(ref_b, ref_b, ("x", 8), x_dev), has(own, 0)))
    ref = slab.at[own, 0, pl.ds(0, 64)]
    sent.append((copy(ref, ref, ("x", 0), x_dev), has(own, 0)))
    sent.append((copy(ref_l, ref_l, ("x", 9), x_dev), jnp.logical_and(low_here, near)))
    for k, ref in ((0, slab.at[own, 0]), (2, ref_l)):
        sent.append((copy(ref, ref, ("c", 0, k), c_dev), None))

    x_wait(0)
    c_send(0, 1)

    def g_units(t, hop):
        for w in range(2):
            for d in range(2):
                if t < 4 or w == d:
                    o = mod8((hop - t) if d == 0 else (t - hop))
                    yield ptr.at[o, pl.ds(128 * w, 128)], ("g", d, t - 1, w), z_dev[d]

    def g_send(t):
        for ref, key, dev in g_units(t, 1):
            send(ref, ref, key, dev)

    def g_wait(t):
        onward = list(g_units(t + 1, 1)) if t < 3 else list(g_units(4, 1)) if t == 3 else []
        for ref, key, dev in g_units(t, 0):
            arrived(ref, key, dev)
            for out, out_key, out_dev in onward:
                if out_key[1] == key[1] and out_key[3] == key[3]:
                    send(out, out, out_key, out_dev)

    pairs = {0: (0,), 1: (1, 4), 2: (2, 5), 3: (3, 6), 4: (7,)}
    for t in range(1, 5):
        for u in range(4):
            for d in range(2):
                z_wait(d, t, u)
                if t < 4:
                    z_send(d, t + 1, u)
            for p in pairs[t]:
                if u == 0:
                    x_send(p)
                if u % 2:
                    c_send(p, u - 1)
            for i, p in enumerate(pairs[t - 1]):
                if u == (1, 2)[i]:
                    top_slice(p)
            if u == 3 and t >= 2:
                top_combine(pairs[t - 2])
            if u == 3 and t >= 3:
                top_finish(pairs[t - 3])
        for p in pairs[t]:
            x_wait(p)
            c_send(p, 1)
        if t == 3:
            g_send(1)

    top_slice(7)

    for h in range(2):
        xt[h] = jnp.zeros((256, 256), F32)

    def image(i, _):
        b0, b1 = pat[0, 2 * i], pat[0, 2 * i + 1]
        both = pt[i]
        for h in range(2):
            bh = jnp.concatenate([shi[b0, h], shi[b1, h]], axis=0)
            bl = jnp.concatenate([slo[b0, h], slo[b1, h]], axis=0)
            wide = mm(both, bh)
            xt[h] += wide[:256] + wide[256:] + mm(both[:256], bl)
        return 0

    lax.fori_loop(0, 8, image, 0)
    for h in range(2):
        hi, lo = split(xt[h].T)
        xhi[h] = hi
        xlo[h] = lo
    def rel_of(k):
        return ((k + 1) // 2 + 2 * (1 - k % 2)) % 4

    def panel_parts(s, pieces):
        bs = [pat[0, 4 * ((y + rel) % 4) + 2 * ab + s] for rel, ab in pieces]
        total = 0.0
        for h in range(2):
            ah = jnp.concatenate([shi[b, h] for b in bs], axis=0)
            al = jnp.concatenate([slo[b, h] for b in bs], axis=0)
            total = total + (mm(ah, xhi[h]) + mm(ah, xlo[h]) + mm(al, xhi[h]))
        return [total[i * 128 : (i + 1) * 128] for i in range(len(pieces))]

    def diag_parts(s, pieces):
        blocks = [ptr[2 * ((y + rel) % 4) + ab, s * 128 : (s + 1) * 128, :] for rel, ab in pieces]
        ah, al = split(jnp.concatenate(blocks, axis=0))
        total = mm(ah, sphi[...]) + mm(ah, splo[...]) + mm(al, sphi[...])
        return [total[i * 128 : (i + 1) * 128] for i in range(len(pieces))]

    def start(q, parts):
        def far(rels):
            for rel, value in zip(rels, parts(1, [(rel, 1 - xh) for rel in rels])):
                vs[q, rel] = value
                send(vs.at[q, rel], vr.at[q, rel], ("v", q, rel), h_dev)

        def near_y(ks):
            for k, value in zip(ks, parts(0, [(rel_of(k), k % 2) for k in ks])):
                psl[q, k] = value

        near_y((0, 1, 2, 3))
        for d in range(2):
            send(psl.at[q, pl.ds(2 * d, 2)], pr1.at[q, d], ("q", q, d), y_dev[d])
        far((2, 1, 3, 0))
        for rel, value in enumerate(parts(1, [(rel, xh) for rel in range(4)])):
            vo[q, rel, 0] = value[:64]
            vo[q, rel, 1] = value[64:]
        near_y((4, 5, 6, 7))

    def v_add(q, rel):
        arrived(vr.at[q, rel], ("v", q, rel), h_dev)
        vo[q, rel, 0] += vr[q, rel, :64]
        vo[q, rel, 1] += vr[q, rel, 64:]

    def v_first(q):
        v_add(q, 2)
        for d in range(2):
            send(vo.at[q, 2, d], v1.at[q, d], ("v", q, 4 + d), y_dev[d])

    def v_second(q):
        for d, rel in ((0, 1), (1, 3)):
            v_add(q, rel)
            arrived(v1.at[q, d], ("v", q, 4 + d), y_dev[d])
            vo[q, rel, d] += v1[q, d]
            send(vo.at[q, rel], v2.at[q, d], ("v", q, 6 + d), y_dev[d])

    def v_total(q):
        v_add(q, 0)
        for d in range(2):
            arrived(v2.at[q, d], ("v", q, 6 + d), y_dev[d])
        return [vo[q, 0, i] + v2[q, 0, i] + v2[q, 1, i] for i in range(2)]

    def u_combine(q):
        for d, slot in ((0, 6), (1, 5)):
            arrived(pr1.at[q, d], ("q", q, d), y_dev[d])
            psl[q, slot] += pr1[q, d, d]
            send(psl.at[q, slot], pr2.at[q, d], ("q", q, 2 + d), y_dev[d])

    def u_across(q):
        for d in range(2):
            arrived(pr2.at[q, d], ("q", q, 2 + d), y_dev[d])
        psl[q, 4] += pr1[q, 1, 0] + pr2[q, 0]
        psl[q, 7] += pr1[q, 0, 1] + pr2[q, 1]
        send(psl.at[q, 7 - 3 * xh], px.at[q], ("q", q, 4), h_dev)

    def u_total(q):
        arrived(px.at[q], ("q", q, 4), h_dev)
        return psl[q, 4 + 3 * xh] + px[q]

    g_wait(1)
    start(0, panel_parts)
    g_wait(2)
    v_first(0)
    u_combine(0)
    top_combine(pairs[3])
    top_finish(pairs[2])
    g_wait(3)
    v_second(0)
    u_across(0)
    top_combine(pairs[4])
    top_finish(pairs[3])
    top_finish(pairs[4])

    def keep(rows, sp):
        out_panel[rows, :] = sp
        hi, lo = split(sp)
        sphi[rows, :] = hi
        splo[rows, :] = lo

    for i, part in enumerate(v_total(0)):
        keep(slice(128 + 64 * i, 192 + 64 * i), part)
    g_wait(4)
    keep(slice(0, 128), u_total(0))
    keep_panel = pltpu.make_async_copy(out_panel, panel_sum, loads.at[2])
    keep_panel.start()
    start(1, diag_parts)
    v_first(1)
    u_combine(1)
    v_second(1)
    u_across(1)
    for p in range(8):
        o = origin(p)
        arrived(xtop.at[o % 4], ("a", p), h_dev, o // 4 == xh)
    for i in range(4):
        out_top[i * 128 : (i + 1) * 128, :] = acc[4 * xh + i] + xtop[i]
    keep_top = pltpu.make_async_copy(out_top, top_sum, loads.at[3])
    keep_top.start()
    for i, part in enumerate(v_total(1)):
        out_diag[128 + 64 * i : 192 + 64 * i, :] = part
    rows = pl.ds(128, 128)
    keep_late = pltpu.make_async_copy(out_diag.at[rows], diag_sum.at[rows], loads.at[6])
    keep_late.start()
    out_diag[:128, :] = u_total(1)
    rows = pl.ds(0, 128)
    keep_diag = pltpu.make_async_copy(out_diag.at[rows], diag_sum.at[rows], loads.at[4])
    keep_diag.start()
    for desc in (keep_panel, keep_top, keep_late, keep_diag):
        desc.wait()
    for desc, cond in sent:
        if cond is None:
            desc.wait_send()
        else:
            pl.when(cond)(desc.wait_send)


def finish(top_in, panel_in, update_in, diag_in, top_out, panel_out, diag_out, top, sp, upd, diag, sems):
    pairs = ((top_in, top), (panel_in, sp), (update_in, upd), (diag_in, diag))
    loads = [pltpu.make_async_copy(a, b, sems.at[i]) for i, (a, b) in enumerate(pairs)]
    for load in loads:
        load.start()
    loads[0].wait()
    stores = [pltpu.make_async_copy(top, top_out, sems.at[4])]
    stores[0].start()
    loads[1].wait()
    sp[...] = -sp[...]
    stores.append(pltpu.make_async_copy(sp, panel_out.at[0], sems.at[5]))
    stores[1].start()
    loads[2].wait()
    loads[3].wait()
    upd[...] = diag[0] + upd[...]
    stores.append(pltpu.make_async_copy(upd, diag_out.at[0], sems.at[6]))
    stores[2].start()
    for store in stores:
        store.wait()


def per_device(top_inverse, pattern, panel, diag_inverse):
    hbm = pl.BlockSpec(memory_space=pl.ANY)
    smem = pl.BlockSpec(memory_space=pltpu.SMEM)
    dma, f32, b16 = pltpu.SemaphoreType.DMA, lambda *n: pltpu.VMEM(n, F32), lambda *n: pltpu.VMEM(n, BF16)
    shape = lambda *n: jax.ShapeDtypeStruct(n, F32)
    counts = ((2, 4, 4), (10,), (8, 3), (8, 4), (2, 5), (2, 8), (2, 4, 2), (8,), (1,))
    sums = pl.pallas_call(
        kernel,
        out_shape=(shape(512, 128), shape(256, 256), shape(256, 256)),
        in_specs=[smem, hbm, hbm],
        out_specs=(hbm, hbm, hbm),
        scratch_shapes=[
            f32(2, 256, 128), f32(256, 128), f32(1, 2048, 256), f32(512, 128), f32(256, 256), f32(256, 256),
            f32(32, 2, 128, 256), b16(32, 2, 128, 256), b16(32, 2, 128, 256),
            b16(2, 256, 256), f32(8, 256, 256), b16(8, 512, 256),
            f32(2, 256, 256), b16(2, 256, 256), b16(2, 256, 256),
            f32(8, 8, 64, 128), f32(8, 2, 2, 64, 128), f32(8, 2, 64, 128),
            f32(8, 128, 128), f32(4, 128, 128),
            f32(2, 8, 128, 256), f32(2, 2, 2, 128, 256), f32(2, 2, 128, 256), f32(2, 128, 256),
            f32(2, 4, 128, 256), f32(2, 4, 2, 64, 256), f32(2, 4, 128, 256),
            f32(2, 2, 64, 256), f32(2, 2, 2, 64, 256),
            b16(256, 256), b16(256, 256),
            dma((7,)), *(dma(n) for n in counts for _ in range(2)),
        ],
        compiler_params=pltpu.CompilerParams(
            collective_id=0, has_side_effects=True, vmem_limit_bytes=60 * 2**20
        ),
    )(pattern, top_inverse, panel)
    return pl.pallas_call(
        finish,
        out_shape=(shape(512, 128), shape(1, 256, 256), shape(1, 256, 256)),
        in_specs=[hbm] * 4,
        out_specs=(hbm, hbm, hbm),
        scratch_shapes=[f32(512, 128), f32(256, 256), f32(256, 256), f32(1, 256, 256), dma((7,))],
    )(*sums, diag_inverse)


def solution(mesh):
    return jax.shard_map(
        per_device,
        mesh=mesh,
        in_specs=(P("row", ("leaf", "col")), P("leaf", None), P("leaf", None, "col"), P("leaf", "row", "col")),
        out_specs=(P("row", ("leaf", "col")), P("leaf", "row", "col"), P("leaf", "row", "col")),
        check_vma=False,
    )
```
